256 devices in a mesh: doc: 32 (over y, x, core), term: 4 (over z_lo), pair: 2 (over z_hi).
Axes of the slice: x: 4, y: 4, z: 8 (z_hi: 2, z_lo: 4; z = z_hi * 4 + z_lo), core: 2. Of those that a mesh axis runs over, the one named last changes fastest.
Arguments:
- counts: int32 [64, 16, 128, 128], P('doc', 'term'), may hold values from 0 to 11
- block_ids: int32 [64, 16], P('doc', 'term'), may hold values from 0 to 8191, as said below
- live_slots: int32 [64, 16], P('doc', 'term'), may hold values 0 or 1
- lengths: int32 [8192], P('doc'), may hold values from 1 to 24528, as said below
- pairs: int32 [4096, 2], P(('doc', 'pair')), may hold values from 0 to 63, as said below
- pair_count: int32 [64], P(('doc', 'pair')), may hold values from 1 to 64, as said below
Outputs:
- gram: float32 [4096, 128, 128], P(('doc', 'pair'), 'term')
The draws below stay inside these ranges and needn't reach their ends.
Inputs may be any that keep to these rules, and one draw needn't show every extreme that they name: `block_ids`: columns s * 4 to (s + 1) * 4 - 1 hold term blocks of the s-th of 4 equal ranges of the 8192 blocks, distinct within one document block and range. `lengths`: document b * 128 + r has a length of the sum of counts[b, s, r, t] over all slots s and all t plus tokens outside its blocks: 1 to 2000 of them for every document but the last, whose length is exactly 24528. `pairs`: the left block of row k belongs to doc index k // 128. Rows k with k % 64 < pair_count[k // 64] are live; some entry equals 64.
All inputs are finite; a program needn't handle non-finite values. No bound on the sum of `live_slots` on one device may be relied on, other than what follows from the above.
Results may differ from the reference program's by a relative error of at most 0.0014.
Values may be sent and summed in bfloat16 or wider, within the bound.
No kernel may reach another device: no remote copies, remote signals or barrier semaphores. Data moves between devices by JAX's collectives and lax.ppermute only.
A program may use at most 64 MiB of HBM per device.

```python
import jax
import jax.numpy as jnp
from jax import lax

V = 1048576
TBLK = 128
DOCBLK = 128
DB_DEV = 2
TERM_BLOCK_SLOTS = 4
PAIR_DEV = 64
TERM_BLOCKS = 8192
NDB = 64
DOCS = 8192
TSLOTS = 16
NPAIRS = 4096
N_DOC = 32
N_TERM = 4
N_PAIR = 2


def draw_block_ids(key, part):
    covered_blocks = V // TBLK // N_TERM
    perm_keys = jax.random.split(jax.random.fold_in(key, 21), N_TERM)
    ordering = jax.vmap(lambda part_key: jax.random.permutation(part_key, covered_blocks))(perm_keys)
    ranking_order = jnp.argsort(ordering, axis=1).astype(jnp.int32)
    extra_score = jnp.where(ranking_order < 2 * TERM_BLOCK_SLOTS, 2 ** 18, 0).astype(jnp.int32)
    jitter_score = jax.random.randint(jax.random.fold_in(key, 22), (NDB, N_TERM, covered_blocks), 0, 2 ** 18)
    complete_score = (jitter_score + extra_score[None]) * covered_blocks + jnp.arange(covered_blocks, dtype=jnp.int32)
    picked = lax.top_k(complete_score, TERM_BLOCK_SLOTS)[1].astype(jnp.int32)
    global_ids = picked + (jnp.arange(N_TERM, dtype=jnp.int32) * covered_blocks)[None, :, None]
    return global_ids.reshape(NDB, N_TERM * TERM_BLOCK_SLOTS).astype(jnp.int32)


def count_grid(key):
    slot_total = TERM_BLOCK_SLOTS * N_TERM
    grid_shape = (NDB, slot_total, DOCBLK, TBLK)
    slot_blocks = draw_block_ids(key, 0)
    term_level = jax.random.randint(jax.random.fold_in(key, 14), (TERM_BLOCKS, TBLK), 300, 1001)
    slot_level = jax.random.randint(jax.random.fold_in(key, 15), (NDB, slot_total), 500, 1001)
    level = term_level[slot_blocks] * slot_level[:, :, None] // 1000
    doc_index = jnp.arange(NDB, dtype=jnp.int32)[:, None, None, None] * DOCBLK + jnp.arange(DOCBLK, dtype=jnp.int32)[None, None, :, None]
    thresh = level[:, :, None, :] * (DOCS + 2 * doc_index) // (2 * DOCS)
    coin_flip = jax.random.randint(jax.random.fold_in(key, 11), grid_shape, 0, 1000)
    ceiling = jax.random.randint(jax.random.fold_in(key, 12), grid_shape, 2, 13)
    count_value = jax.random.randint(jax.random.fold_in(key, 13), grid_shape, 1, ceiling)
    return jnp.where(coin_flip < thresh, count_value, 0).astype(jnp.int32)


def draw_counts(key, part):
    return count_grid(key)


def draw_lengths(key, part):
    grid = count_grid(key)
    inside = jnp.sum(grid, axis=(1, 3)).reshape(DOCS)
    block_top = jax.random.randint(jax.random.fold_in(key, 32), (NDB,), 2, 2002)
    doc_top = jnp.repeat(block_top, DOCBLK)
    outside = jax.random.randint(jax.random.fold_in(key, 31), (DOCS,), 1, doc_top)
    top_length = 11 * TERM_BLOCK_SLOTS * N_TERM * TBLK + 2000
    outside = outside.at[DOCS - 1].set(top_length - inside[DOCS - 1])
    return (inside + outside).astype(jnp.int32)


def draw_pairs(key, part):
    row_index = jnp.arange(NPAIRS, dtype=jnp.int32)
    owner_index = row_index // (PAIR_DEV * N_PAIR)
    left_block = owner_index * DB_DEV + jax.random.randint(jax.random.fold_in(key, 41), (NPAIRS,), 0, DB_DEV)
    right_block = jax.random.randint(jax.random.fold_in(key, 42), (NPAIRS,), 0, NDB)
    return jnp.stack([left_block, right_block], axis=1).astype(jnp.int32)


def draw_pair_count(key, part):
    heavy_side = jax.random.randint(jax.random.fold_in(key, 51), (N_DOC,), 0, N_PAIR)
    heavy_count = jax.random.randint(jax.random.fold_in(key, 52), (N_DOC,), 3 * PAIR_DEV // 4, PAIR_DEV + 1)
    heavy_count = heavy_count.at[0].set(PAIR_DEV)
    light_count = jax.random.randint(jax.random.fold_in(key, 53), (N_DOC, N_PAIR), 1, PAIR_DEV // 4 + 1)
    side_index = jnp.arange(N_PAIR, dtype=jnp.int32)[None, :]
    return jnp.where(side_index == heavy_side[:, None], heavy_count[:, None], light_count).reshape(-1).astype(jnp.int32)


def place_ends(drawn, own_key, low, largest):
    spot = [jax.random.randint(jax.random.fold_in(own_key, axis), (), 0, length) for axis, length in enumerate(drawn.shape)]
    longest = drawn.shape.index(max(drawn.shape))
    beside = spot[:longest] + [(spot[longest] + 1) % drawn.shape[longest]] + spot[longest + 1:]
    return drawn.at[tuple(spot)].set(low).at[tuple(beside)].set(largest)


def setup_inputs(seed: int = 0) -> dict:
    splits = jax.random.split(jax.random.key(seed), 7)
    counts = draw_counts(jax.random.fold_in(splits[6], 71), 0)
    block_ids = draw_block_ids(jax.random.fold_in(splits[6], 71), 0)
    live_slots = place_ends((jax.random.randint(splits[2], (NDB, TSLOTS), 0, 4) < 3).astype(jnp.int32), jax.random.fold_in(splits[2], 1), 0, 1)
    lengths = draw_lengths(jax.random.fold_in(splits[6], 71), 0)
    pairs = draw_pairs(jax.random.fold_in(splits[6], 71), 0)
    pair_count = draw_pair_count(jax.random.fold_in(splits[6], 71), 0)
    return dict(counts=counts, block_ids=block_ids, live_slots=live_slots, lengths=lengths, pairs=pairs, pair_count=pair_count)


saturation = 1.2
length_weight = 0.75
epsilon = 1e-06

def reference(counts, block_ids, live_slots, lengths, pairs, pair_count):
    present = (counts > 0) & (live_slots[:, :, None, None] > 0)
    col_docs = lax.optimization_barrier(jnp.sum(present.astype(jnp.float32), axis=2))
    doc_freq = jnp.zeros((TERM_BLOCKS, TBLK), jnp.float32).at[block_ids.reshape(-1)].add(col_docs.reshape(-1, TBLK))
    len_float = lengths.astype(jnp.float32)
    avg_len = jnp.sum(len_float) / DOCS
    inv_freq = jnp.log(1.0 + (DOCS - doc_freq + 0.5) / (doc_freq + 0.5))
    slot_freq = inv_freq[block_ids]
    len_scale = 1.0 - length_weight + length_weight * len_float.reshape(NDB, 1, DOCBLK, 1) / avg_len
    term_freq = counts.astype(jnp.float32)
    weight = jnp.where(present, slot_freq[:, :, None, :] * term_freq * (saturation + 1.0) / (term_freq + saturation * len_scale), 0.0)
    square_sum = lax.optimization_barrier(jnp.sum(weight * weight, axis=(1, 3)))
    normalized = (weight * lax.rsqrt(square_sum + epsilon)[:, None, :, None]).astype(jnp.bfloat16)
    row_index = jnp.arange(NPAIRS, dtype=jnp.int32)
    live_pair = row_index % PAIR_DEV < pair_count[row_index // PAIR_DEV]

    def one_pair(item):
        pair_row, live_flag = item
        left_tiles = normalized[pair_row[0]].astype(jnp.float32)
        right_tiles = normalized[pair_row[1]].astype(jnp.float32)
        matches = (block_ids[pair_row[0]][:, None] == block_ids[pair_row[1]][None, :]).astype(jnp.float32)
        aligned = jnp.einsum('ij,jet->iet', matches, right_tiles)
        gram_tile = jnp.einsum('idt,iet->de', left_tiles, aligned)
        return jnp.where(live_flag, gram_tile, 0.0)
    return lax.map(one_pair, (pairs, live_pair))
```

```python
import jax
import jax.numpy as jnp
from jax import lax
from jax.experimental import pallas as pl
from jax.experimental.pallas import tpu as pltpu
from jax.sharding import PartitionSpec as P

PAIRS_PER_STEP = 4
CHUNK = 16
GRAM_SCALE = 32768.0

saturation = 1.2
length_weight = 0.75
epsilon = 1e-06


def gram_kernel(left_sel, right_sel, own_ids, all_ids, live, left_ref, length_ref, norm_ref, *refs):
    tile_refs = refs[:PAIRS_PER_STEP]
    out_ref = refs[PAIRS_PER_STEP]
    slots = tile_refs[0].shape[1]
    step = pl.program_id(0)
    for p in range(PAIRS_PER_STEP):
        k = step * PAIRS_PER_STEP + p
        left = left_sel[k]
        right = right_sel[k]
        len_row = length_ref[pl.ds(right, 1), :]
        parts = []
        for i in range(slots):
            wanted = own_ids[left * slots + i]
            found = jnp.int32(0)
            place = jnp.int32(0)
            for j in range(slots):
                same = all_ids[right * slots + j] == wanted
                found = jnp.where(same, 1, found)
                place = jnp.where(same, j, place)
            c = tile_refs[p][0, place].astype(jnp.float32)
            f = c / (c + len_row)
            parts.append((f * found.astype(jnp.float32)).astype(jnp.bfloat16))
        right_tile = jnp.concatenate(parts, axis=0)
        gram = jnp.dot(left_ref[left], right_tile, preferred_element_type=jnp.float32)
        scale = norm_ref[pl.ds(right, 1), :] * (live[k].astype(jnp.float32) * GRAM_SCALE)
        out_ref[p] = gram * scale


def gram_chunk(left_sel, right_sel, own_ids, all_ids, live, left_tiles, len_rows, norm_rows, tiles):
    pairs = left_sel.shape[0]
    blocks, slots, terms, rows = tiles.shape
    tile_specs = [
        pl.BlockSpec(
            (1, slots, terms, rows),
            lambda s, ls, rs, oi, ai, lv, p=p: (rs[s * PAIRS_PER_STEP + p], 0, 0, 0),
        )
        for p in range(PAIRS_PER_STEP)
    ]
    whole = lambda a: pl.BlockSpec(a.shape, lambda s, *_: (0,) * a.ndim)
    return pl.pallas_call(
        gram_kernel,
        grid_spec=pltpu.PrefetchScalarGridSpec(
            num_scalar_prefetch=5,
            grid=(pairs // PAIRS_PER_STEP,),
            in_specs=[whole(left_tiles), whole(len_rows), whole(norm_rows)] + tile_specs,
            out_specs=pl.BlockSpec((PAIRS_PER_STEP, rows, rows), lambda s, *_: (s, 0, 0)),
        ),
        out_shape=jax.ShapeDtypeStruct((pairs, rows, rows), jnp.float32),
        name="gram",
    )(
        left_sel, right_sel, own_ids, all_ids, live, left_tiles, len_rows, norm_rows,
        *([tiles] * PAIRS_PER_STEP),
    )


def shards(counts, block_ids, live_slots, lengths, pairs, pair_count):
    blocks, slots, rows, terms = counts.shape
    n_doc = lax.axis_size("doc")
    n_term = lax.axis_size("term")
    term_at = lax.axis_index("term")
    docs_all = lengths.shape[0] * n_doc
    own_slots = blocks * slots

    live_counts = jnp.where(live_slots[:, :, None, None] > 0, counts, 0)
    send_tiles = jnp.swapaxes(live_counts, 2, 3).astype(jnp.bfloat16)
    all_tiles = lax.all_gather(send_tiles, "doc", axis=0, tiled=True)

    col_docs = jnp.sum((live_counts > 0).astype(jnp.int32), axis=2).reshape(own_slots, terms)
    own_ids = block_ids.reshape(-1)
    small = jnp.concatenate(
        [
            col_docs,
            lengths.reshape(blocks, rows),
            jnp.pad(own_ids, (0, terms - own_slots)).reshape(1, terms),
        ],
        axis=0,
    )
    small_all = lax.all_gather(small, "doc", axis=0)
    col_all = small_all[:, :own_slots].reshape(n_doc * own_slots, terms)
    len_all = small_all[:, own_slots : own_slots + blocks].reshape(n_doc * blocks, rows)
    all_ids = small_all[:, own_slots + blocks, :own_slots].reshape(-1)

    same_ids = (own_ids[:, None] == all_ids[None, :]).astype(jnp.bfloat16)
    doc_freq = jnp.dot(same_ids, col_all.astype(jnp.bfloat16), preferred_element_type=jnp.float32)
    inv_freq = jnp.log(1.0 + (docs_all - doc_freq + 0.5) / (doc_freq + 0.5))
    idf = (inv_freq * (saturation + 1.0)).reshape(blocks, slots, 1, terms)
    avg_len = jnp.sum(len_all).astype(jnp.float32) / docs_all
    len_rows = saturation * (
        1.0 - length_weight + length_weight * len_all.astype(jnp.float32) / avg_len
    )
    own_len = saturation * (
        1.0 - length_weight + length_weight * lengths.astype(jnp.float32) / avg_len
    )
    own_c = live_counts.astype(jnp.float32)
    weight = idf * own_c / (own_c + own_len.reshape(blocks, 1, rows, 1))
    square_sum = lax.psum(jnp.sum(weight * weight, axis=(1, 3)), "term")
    norm = lax.rsqrt(square_sum + epsilon)
    left_tiles = (weight * idf * norm[:, None, :, None]).astype(jnp.bfloat16)
    left_tiles = jnp.swapaxes(left_tiles, 1, 2).reshape(blocks, rows, slots * terms)
    norm_rows = lax.all_gather(norm, "doc", axis=0, tiled=True)

    left_sel = pairs[:, 0] - lax.axis_index("doc") * blocks
    right_sel = pairs[:, 1]
    pair_slots = pairs.shape[0]
    live = (jnp.arange(pair_slots, dtype=jnp.int32) < pair_count[0]).astype(jnp.int32)
    rows_each = rows // n_term
    results = []
    for first in range(0, pair_slots, CHUNK):
        span = slice(first, first + CHUNK)
        grams = gram_chunk(
            left_sel[span], right_sel[span], own_ids, all_ids, live[span],
            left_tiles, len_rows, norm_rows, all_tiles,
        )
        cut = lambda to: lax.dynamic_slice_in_dim(grams, to * rows_each, rows_each, 1)
        total = cut(term_at)
        for shift in range(1, n_term):
            message = cut((term_at + shift) % n_term).astype(jnp.float16)
            got = lax.ppermute(
                message, "term", [(a, (a + shift) % n_term) for a in range(n_term)]
            )
            total = total + got.astype(jnp.float32)
        results.append(total * (1.0 / GRAM_SCALE))
    return jnp.concatenate(results, axis=0)


def solution(mesh):
    in_specs = (
        P("doc", "term", None, None),
        P("doc", "term"),
        P("doc", "term"),
        P("doc"),
        P(("doc", "pair"), None),
        P(("doc", "pair")),
    )
    out_specs = P(("doc", "pair"), "term", None)
    return jax.shard_map(shards, mesh=mesh, in_specs=in_specs, out_specs=out_specs, check_vma=False)
```

```python
import jax
import jax.numpy as jnp
from jax import lax
from jax.experimental import pallas as pl
from jax.experimental.pallas import tpu as pltpu
from jax.sharding import PartitionSpec as P


SIDE = 4
CORES = 2
PAIRS_PER_STEP = 4
CHUNKS = (16, 16, 16, 16)
GRAM_SCALE = 32768.0

saturation = 1.2
length_weight = 0.75
epsilon = 1e-06


def doc_of(y, x, core):
    return ((y % SIDE) * SIDE + x % SIDE) * CORES + core % CORES


def doc_moves(dy, dx, dcore):
    return [
        (doc_of(y + dy, x + dx, c + dcore), doc_of(y, x, c))
        for y in range(SIDE)
        for x in range(SIDE)
        for c in range(CORES)
    ]


def gather_small(value):
    value = value[None]
    for move in ((0, 0, 1), (0, 1, 0), (0, 2, 0), (1, 0, 0), (2, 0, 0)):
        value = jnp.concatenate([value, lax.ppermute(value, "doc", doc_moves(*move))], axis=0)
    return value


def swap_term(value, bit, n_term):
    return lax.ppermute(value, "term", [(a, a ^ bit) for a in range(n_term)])


def gram_kernel(left_sel, right_sel, right_rel, own_ids, all_ids, live, left_ref, idf_ref, length_ref, norm_ref, *refs):
    tile_refs = refs[:PAIRS_PER_STEP]
    keep_ref, send_ref = refs[PAIRS_PER_STEP:]
    slots = tile_refs[0].shape[1]
    half = keep_ref.shape[1]
    step = pl.program_id(0)
    for p in range(PAIRS_PER_STEP):
        k = step * PAIRS_PER_STEP + p
        left = left_sel[k]
        right = right_rel[k]
        len_row = length_ref[pl.ds(right, 1), :]
        norm_row = norm_ref[pl.ds(right, 1), :] * (live[k].astype(jnp.float32) * GRAM_SCALE)
        parts = []
        for i in range(slots):
            wanted = own_ids[left * slots + i]
            found = jnp.int32(0)
            place = jnp.int32(0)
            for j in range(slots):
                same = all_ids[right * slots + j] == wanted
                found = jnp.where(same, 1, found)
                place = jnp.where(same, j, place)
            c = tile_refs[p][0, place].astype(jnp.float32)
            factor = (norm_row * found.astype(jnp.float32)) / (c + len_row)
            parts.append((c * idf_ref[left * slots + i] * factor).astype(jnp.bfloat16))
        right_tile = jnp.concatenate(parts, axis=0)
        gram = jnp.dot(left_ref[left], right_tile, preferred_element_type=jnp.float32)
        keep_ref[p] = gram[:half]
        send_ref[p] = gram[half:]


def gram_chunk(left_sel, right_sel, right_rel, own_ids, all_ids, live, left_tiles, idf_tiles, len_rows, norm_rows, tiles):
    pairs = left_sel.shape[0]
    blocks, slots, terms, rows = tiles.shape
    tile_specs = [
        pl.BlockSpec(
            (1, slots, terms, rows),
            lambda s, ls, rs, *_, p=p: (rs[s * PAIRS_PER_STEP + p], 0, 0, 0),
        )
        for p in range(PAIRS_PER_STEP)
    ]
    whole = lambda a: pl.BlockSpec(a.shape, lambda s, *_: (0,) * a.ndim)
    half_spec = pl.BlockSpec((PAIRS_PER_STEP, rows // 2, rows), lambda s, *_: (s, 0, 0))
    half_shape = jax.ShapeDtypeStruct((pairs, rows // 2, rows), jnp.float32)
    return pl.pallas_call(
        gram_kernel,
        grid_spec=pltpu.PrefetchScalarGridSpec(
            num_scalar_prefetch=6,
            grid=(pairs // PAIRS_PER_STEP,),
            in_specs=[whole(a) for a in (left_tiles, idf_tiles, len_rows, norm_rows)] + tile_specs,
            out_specs=[half_spec, half_spec],
        ),
        out_shape=[half_shape, half_shape],
        name="gram",
    )(
        left_sel, right_sel, right_rel, own_ids, all_ids, live,
        left_tiles, idf_tiles, len_rows, norm_rows, *([tiles] * PAIRS_PER_STEP),
    )


def shards(counts, block_ids, live_slots, lengths, pairs, pair_count):
    blocks, slots, rows, terms = counts.shape
    n_doc = lax.axis_size("doc")
    n_term = lax.axis_size("term")
    doc_at = lax.axis_index("doc")
    term_at = lax.axis_index("term")
    docs_all = lengths.shape[0] * n_doc
    own_slots = blocks * slots

    live_counts = jnp.where(live_slots[:, :, None, None] > 0, counts, 0)
    send_tiles = jnp.swapaxes(live_counts, 2, 3).astype(jnp.bfloat16)
    all_tiles = lax.all_gather(send_tiles, "doc", axis=0, tiled=True)

    col_docs = jnp.sum((live_counts > 0).astype(jnp.int32), axis=2).reshape(own_slots, terms)
    own_ids = block_ids.reshape(-1)
    small = jnp.concatenate(
        [
            col_docs,
            lengths.reshape(blocks, rows),
            jnp.pad(own_ids, (0, terms - own_slots)).reshape(1, terms),
        ],
        axis=0,
    )
    small_all = gather_small(small)
    col_all = small_all[:, :own_slots].reshape(n_doc * own_slots, terms)
    len_all = small_all[:, own_slots : own_slots + blocks].reshape(n_doc * blocks, rows)
    all_ids = small_all[:, own_slots + blocks, :own_slots].reshape(-1)

    same_ids = (own_ids[:, None] == all_ids[None, :]).astype(jnp.bfloat16)
    doc_freq = jnp.dot(same_ids, col_all.astype(jnp.bfloat16), preferred_element_type=jnp.float32)
    inv_freq = jnp.log(1.0 + (docs_all - doc_freq + 0.5) / (doc_freq + 0.5))
    idf = inv_freq * (saturation + 1.0)
    avg_len = jnp.sum(len_all).astype(jnp.float32) / docs_all
    len_rows = saturation * (
        1.0 - length_weight + length_weight * len_all.astype(jnp.float32) / avg_len
    )
    own_len = saturation * (
        1.0 - length_weight + length_weight * lengths.astype(jnp.float32) / avg_len
    )
    own_c = live_counts.astype(jnp.float32)
    weight = (
        idf.reshape(blocks, slots, 1, terms) * own_c / (own_c + own_len.reshape(blocks, 1, rows, 1))
    )
    square_sum = jnp.sum(weight * weight, axis=(1, 3))
    square_sum = square_sum + swap_term(square_sum, 1, n_term)
    square_sum = square_sum + swap_term(square_sum, 2, n_term)
    norm = lax.rsqrt(square_sum + epsilon)
    norm_rows = gather_small(norm).reshape(n_doc * blocks, rows)
    left_tiles = (weight * norm[:, None, :, None]).astype(jnp.bfloat16)
    owners = term_at ^ jnp.array([0, 2, 1, 3], jnp.int32)
    left_tiles = left_tiles.reshape(blocks, slots, n_term, rows // n_term, terms)[:, :, owners]
    left_tiles = left_tiles.reshape(blocks, slots, rows, terms)
    left_tiles = jnp.swapaxes(left_tiles, 1, 2).reshape(blocks, rows, slots * terms)
    idf_tiles = jnp.broadcast_to(idf[:, :, None], (own_slots, terms, rows))

    left_sel = pairs[:, 0] - doc_at * blocks
    right_sel = pairs[:, 1]
    right_doc = right_sel // blocks
    from_y = (right_doc // (SIDE * CORES) - doc_at // (SIDE * CORES)) % SIDE
    from_x = (right_doc // CORES - doc_at // CORES) % SIDE
    from_core = (right_doc - doc_at) % CORES
    right_rel = ((from_y * SIDE + from_x) * CORES + from_core) * blocks + right_sel % blocks
    pair_slots = pairs.shape[0]
    live = (jnp.arange(pair_slots, dtype=jnp.int32) < pair_count[0]).astype(jnp.int32)
    part = rows // n_term
    results = []
    first = 0
    for size in CHUNKS:
        span = slice(first, first + size)
        first += size
        keep, send = gram_chunk(
            left_sel[span], right_sel[span], right_rel[span], own_ids, all_ids, live[span],
            left_tiles, idf_tiles, len_rows, norm_rows, all_tiles,
        )
        near = swap_term(send.astype(jnp.float16), 1, n_term)
        pass_on = keep[:, part:] + near[:, part:].astype(jnp.float32)
        far = swap_term(pass_on.astype(jnp.float16), 2, n_term)
        total = keep[:, :part] + near[:, :part].astype(jnp.float32) + far.astype(jnp.float32)
        results.append(total * (1.0 / GRAM_SCALE))
    return jnp.concatenate(results, axis=0)


def solution(mesh):
    in_specs = (
        P("doc", "term", None, None),
        P("doc", "term"),
        P("doc", "term"),
        P("doc"),
        P(("doc", "pair"), None),
        P(("doc", "pair")),
    )
    out_specs = P(("doc", "pair"), "term", None)
    return jax.shard_map(shards, mesh=mesh, in_specs=in_specs, out_specs=out_specs, check_vma=False)
```

```python
import jax
import jax.numpy as jnp
from jax import lax
from jax.experimental import pallas as pl
from jax.experimental.pallas import tpu as pltpu
from jax.sharding import PartitionSpec as P


SIDE = 4
CORES = 2
UNROLL = 4
CHUNKS = (16, 24, 24)
GRAM_SCALE = 32.0

saturation = 1.2
length_weight = 0.75
epsilon = 1e-06


def doc_of(y, x, core):
    return ((y % SIDE) * SIDE + x % SIDE) * CORES + core % CORES


def permute_doc(value, source):
    moves = [
        (doc_of(*source(y, x, c)), doc_of(y, x, c))
        for y in range(SIDE)
        for x in range(SIDE)
        for c in range(CORES)
    ]
    return lax.ppermute(value, "doc", moves)


def from_shift(value, dy, dx, dcore):
    return permute_doc(value, lambda y, x, c: (y + dy, x + dx, c + dcore))


def from_ring(value, phase, shift):
    def source(y, x, c):
        return (y, x + shift, c) if c == phase else (y + shift, x, c)

    return permute_doc(value, source)


def gather_small(value):
    value = value[None]
    for move in ((0, 0, 1), (0, 1, 0), (0, 2, 0), (1, 0, 0), (2, 0, 0)):
        value = jnp.concatenate([value, from_shift(value, *move)], axis=0)
    return value


def gather_tiles(tiles):
    half = tiles.shape[0] * SIDE // 2
    ring = jnp.concatenate([tiles] + [from_ring(tiles, 0, s) for s in (1, 2, 3)], axis=0)
    ahead = from_ring(ring, 1, 1)
    behind = from_ring(ring, 1, 3)
    across_low = from_ring(ahead[:half], 1, 1)
    across_high = from_ring(behind[half:], 1, 3)
    own = [ring, ahead, behind, across_low, across_high]
    return own + [from_shift(piece, 0, 0, 1) for piece in own]


def place_right(right_sel, doc_at, blocks):
    doc = right_sel // blocks
    core = doc % CORES
    dx = (doc // CORES - doc_at // CORES) % SIDE
    dy = (doc // (SIDE * CORES) - doc_at // (SIDE * CORES)) % SIDE
    dcore = (doc - doc_at) % CORES
    inner = jnp.where(core == 0, dx, dy)
    outer = jnp.where(core == 0, dy, dx)
    piece = jnp.where(
        outer == 0, 0, jnp.where(outer == 1, 1, jnp.where(outer == 3, 2, 3 + inner // (SIDE // 2)))
    )
    spot = jnp.where(outer == 2, inner % (SIDE // 2), inner) * blocks + right_sel % blocks
    relative = ((dy * SIDE + dx) * CORES + dcore) * blocks + right_sel % blocks
    return piece + dcore * 5, spot, relative


def swap_term(value, bit, n_term):
    return lax.ppermute(value, "term", [(a, a ^ bit) for a in range(n_term)])


def gram_chunk(first, size, select, own_ids, all_ids, left_tiles, idf_tiles, len_rows, pieces):
    _, slots, terms, rows = pieces[0].shape
    half = rows // 2

    def kernel(sel_ref, own_ref, ids_ref, left_ref, idf_ref, length_ref, *refs):
        piece_refs = refs[: len(pieces)]
        keep_ref, send_ref, tile_buf, arrived = refs[len(pieces) :]

        def fetch(k, carry):
            piece = sel_ref[2, first + k]
            spot = sel_ref[3, first + k]
            for p, ref in enumerate(piece_refs):

                @pl.when(piece == p)
                def _():
                    pltpu.make_async_copy(ref.at[spot], tile_buf.at[k], arrived.at[k]).start()

            return carry

        lax.fori_loop(0, size, fetch, 0)

        def multiply(step, carry):
            for p in range(UNROLL):
                k = step * UNROLL + p
                pltpu.make_async_copy(piece_refs[0].at[0], tile_buf.at[k], arrived.at[k]).wait()
            for p in range(UNROLL):
                k = step * UNROLL + p
                left = sel_ref[0, first + k]
                right = sel_ref[1, first + k]
                len_row = length_ref[pl.ds(right, 1), :]
                parts = []
                for i in range(slots):
                    wanted = own_ref[left * slots + i]
                    found = jnp.int32(0)
                    place = jnp.int32(0)
                    for j in range(slots):
                        same = ids_ref[right * slots + j] == wanted
                        found = jnp.where(same, 1, found)
                        place = jnp.where(same, j, place)
                    c = tile_buf[k, place].astype(jnp.float32)
                    factor = found.astype(jnp.float32) / (c + len_row)
                    parts.append((c * idf_ref[left * slots + i] * factor).astype(jnp.bfloat16))
                right_tile = jnp.concatenate(parts, axis=0)
                gram = jnp.dot(left_ref[left], right_tile, preferred_element_type=jnp.float32)
                keep_ref[k] = gram[:half]
                send_ref[k] = gram[half:]
            return carry

        lax.fori_loop(0, size // UNROLL, multiply, 0)

    smem = pl.BlockSpec(memory_space=pltpu.SMEM)
    vmem = pl.BlockSpec(memory_space=pltpu.VMEM)
    anywhere = pl.BlockSpec(memory_space=pl.ANY)
    half_shape = jax.ShapeDtypeStruct((size, half, rows), jnp.float32)
    return pl.pallas_call(
        kernel,
        in_specs=[smem] * 3 + [vmem] * 3 + [anywhere] * len(pieces),
        out_specs=[vmem, vmem],
        out_shape=[half_shape, half_shape],
        scratch_shapes=[
            pltpu.VMEM((size, slots, terms, rows), jnp.bfloat16),
            pltpu.SemaphoreType.DMA((size,)),
        ],
        name="gram",
    )(select, own_ids, all_ids, left_tiles, idf_tiles, len_rows, *pieces)


def shards(counts, block_ids, live_slots, lengths, pairs, pair_count):
    blocks, slots, rows, terms = counts.shape
    n_doc = lax.axis_size("doc")
    n_term = lax.axis_size("term")
    doc_at = lax.axis_index("doc")
    term_at = lax.axis_index("term")
    docs_all = lengths.shape[0] * n_doc
    own_slots = blocks * slots

    live_counts = jnp.where(live_slots[:, :, None, None] > 0, counts, 0)
    col_docs = jnp.sum((live_counts > 0).astype(jnp.int32), axis=2).reshape(own_slots, terms)
    own_ids = block_ids.reshape(-1)
    small = jnp.concatenate(
        [
            col_docs,
            lengths.reshape(blocks, rows),
            jnp.pad(own_ids, (0, terms - own_slots)).reshape(1, terms),
        ],
        axis=0,
    )
    small_all = gather_small(small)
    pieces = gather_tiles(jnp.swapaxes(live_counts, 2, 3).astype(jnp.bfloat16))

    col_all = small_all[:, :own_slots].reshape(n_doc * own_slots, terms)
    len_all = small_all[:, own_slots : own_slots + blocks].reshape(n_doc * blocks, rows)
    all_ids = small_all[:, own_slots + blocks, :own_slots].reshape(-1)

    same_ids = (own_ids[:, None] == all_ids[None, :]).astype(jnp.bfloat16)
    doc_freq = jnp.dot(same_ids, col_all.astype(jnp.bfloat16), preferred_element_type=jnp.float32)
    inv_freq = jnp.log(1.0 + (docs_all - doc_freq + 0.5) / (doc_freq + 0.5))
    idf = inv_freq * (saturation + 1.0)
    avg_len = jnp.sum(len_all).astype(jnp.float32) / docs_all
    len_rows = saturation * (
        1.0 - length_weight + length_weight * len_all.astype(jnp.float32) / avg_len
    )
    own_len = saturation * (
        1.0 - length_weight + length_weight * lengths.astype(jnp.float32) / avg_len
    )
    own_c = live_counts.astype(jnp.float32)
    weight = (
        idf.reshape(blocks, slots, 1, terms) * own_c / (own_c + own_len.reshape(blocks, 1, rows, 1))
    )
    square_sum = jnp.sum(weight * weight, axis=(1, 3))
    square_sum = square_sum + swap_term(square_sum, 1, n_term)
    square_sum = square_sum + swap_term(square_sum, 2, n_term)
    norm = lax.rsqrt(square_sum + epsilon)
    norm_rows = gather_small(norm).reshape(n_doc * blocks, rows)
    left_tiles = (weight * (norm * GRAM_SCALE)[:, None, :, None]).astype(jnp.bfloat16)
    owners = term_at ^ jnp.array([0, 2, 1, 3], jnp.int32)
    left_tiles = left_tiles.reshape(blocks, slots, n_term, rows // n_term, terms)[:, :, owners]
    left_tiles = left_tiles.reshape(blocks, slots, rows, terms)
    left_tiles = jnp.swapaxes(left_tiles, 1, 2).reshape(blocks, rows, slots * terms)
    idf_tiles = jnp.broadcast_to(idf[:, :, None], (own_slots, terms, rows))

    left_sel = pairs[:, 0] - doc_at * blocks
    piece, spot, right_rel = place_right(pairs[:, 1], doc_at, blocks)
    select = jnp.stack([left_sel, right_rel, piece, spot])
    live = jnp.arange(pairs.shape[0], dtype=jnp.int32) < pair_count[0]
    part = rows // n_term
    totals = []
    first = 0
    for size in CHUNKS:
        keep, send = gram_chunk(
            first, size, select, own_ids, all_ids, left_tiles, idf_tiles, len_rows, pieces
        )
        first += size
        near = swap_term(send.astype(jnp.float16), 1, n_term)
        pass_on = keep[:, part:] + near[:, part:].astype(jnp.float32)
        far = swap_term(pass_on.astype(jnp.float16), 2, n_term)
        totals.append(keep[:, :part] + near[:, :part].astype(jnp.float32) + far.astype(jnp.float32))
    right_norm = jnp.where(live[:, None], norm_rows[right_rel] * (1.0 / GRAM_SCALE), 0.0)
    return jnp.concatenate(totals, axis=0) * right_norm[:, None, :]


def solution(mesh):
    in_specs = (
        P("doc", "term", None, None),
        P("doc", "term"),
        P("doc", "term"),
        P("doc"),
        P(("doc", "pair"), None),
        P(("doc", "pair")),
    )
    out_specs = P(("doc", "pair"), "term", None)
    return jax.shard_map(shards, mesh=mesh, in_specs=in_specs, out_specs=out_specs, check_vma=False)
```

```python
import jax
import jax.numpy as jnp
from jax import lax
from jax.experimental import pallas as pl
from jax.experimental.pallas import tpu as pltpu
from jax.sharding import PartitionSpec as P


SIDE = 4
CORES = 2
UNROLL = 4
CHUNKS = (16, 24, 24)
GRAM_SCALE = 32.0
SMALL_ROWS = 16
BYTE = 256

saturation = 1.2
length_weight = 0.75
epsilon = 1e-06


def doc_of(y, x, core):
    return ((y % SIDE) * SIDE + x % SIDE) * CORES + core % CORES


def permute_doc(value, source):
    moves = [
        (doc_of(*source(y, x, c)), doc_of(y, x, c))
        for y in range(SIDE)
        for x in range(SIDE)
        for c in range(CORES)
    ]
    return lax.ppermute(value, "doc", moves)


def from_sibling(value):
    return permute_doc(value, lambda y, x, c: (y, x, c + 1))


def from_ring(value, phase, shift):
    def source(y, x, c):
        return (y, x + shift, c) if c == phase else (y + shift, x, c)

    return permute_doc(value, source)


def gather_ring(value, phase):
    return jnp.concatenate([value] + [from_ring(value, phase, s) for s in (1, 2, 3)], axis=0)


def gather_sibling(value):
    return jnp.concatenate([value, from_sibling(value)], axis=0)


def gather_rest(ring):
    half = ring.shape[0] // 2
    ahead = from_ring(ring, 1, 1)
    behind = from_ring(ring, 1, 3)
    across_low = from_ring(ahead[:half], 1, 1)
    across_high = from_ring(behind[half:], 1, 3)
    own = [ring, ahead, behind, across_low, across_high]
    return own + [from_sibling(piece) for piece in own]


def place_right(right_sel, doc_at, blocks):
    doc = right_sel // blocks
    core = doc % CORES
    dx = (doc // CORES - doc_at // CORES) % SIDE
    dy = (doc // (SIDE * CORES) - doc_at // (SIDE * CORES)) % SIDE
    dcore = (doc - doc_at) % CORES
    inner = jnp.where(core == 0, dx, dy)
    outer = jnp.where(core == 0, dy, dx)
    piece = jnp.where(
        outer == 0, 0, jnp.where(outer == 1, 1, jnp.where(outer == 3, 2, 3 + inner // (SIDE // 2)))
    )
    spot = jnp.where(outer == 2, inner % (SIDE // 2), inner)
    relative = ((dcore * SIDE + outer) * SIDE + inner) * blocks + right_sel % blocks
    return piece + dcore * 5, spot, relative


def swap_term(value, bit, n_term):
    return lax.ppermute(value, "term", [(a, a ^ bit) for a in range(n_term)])


def split_bytes(whole):
    return jnp.concatenate([whole // BYTE, whole % BYTE], axis=0)


def gram_chunk(first, size, select, own_ids, all_ids, order, left_tiles, idf_tiles, len_rows, pieces):
    slots = left_tiles.shape[2] // idf_tiles.shape[1]
    terms, rows = idf_tiles.shape[1:]
    n_term = order.shape[0]
    part = rows // n_term

    def kernel(sel_ref, own_ref, ids_ref, order_ref, left_ref, idf_ref, length_ref, *refs):
        piece_refs = refs[: len(pieces)]
        out_ref, tile_buf, arrived = refs[len(pieces) :]

        def fetch(k, carry):
            piece = sel_ref[2, first + k]
            spot = pl.multiple_of(sel_ref[3, first + k], SMALL_ROWS)
            for p, ref in enumerate(piece_refs):

                @pl.when(piece == p)
                def _():
                    pltpu.make_async_copy(
                        ref.at[pl.ds(spot, slots * terms)], tile_buf.at[k], arrived.at[k]
                    ).start()

            return carry

        lax.fori_loop(0, size, fetch, 0)

        def multiply(step, carry):
            for p in range(UNROLL):
                k = step * UNROLL + p
                pltpu.make_async_copy(
                    piece_refs[0].at[pl.ds(0, slots * terms)], tile_buf.at[k], arrived.at[k]
                ).wait()
            for p in range(UNROLL):
                k = step * UNROLL + p
                left = sel_ref[0, first + k]
                right = sel_ref[1, first + k]
                len_row = length_ref[pl.ds(right, 1), :]
                parts = []
                for i in range(slots):
                    wanted = own_ref[left * slots + i]
                    found = jnp.int32(0)
                    place = jnp.int32(0)
                    for j in range(slots):
                        same = ids_ref[right * slots + j] == wanted
                        found = jnp.where(same, 1, found)
                        place = jnp.where(same, j, place)
                    start = pl.multiple_of(place * terms, terms)
                    c = tile_buf[k, pl.ds(start, terms), :].astype(jnp.float32)
                    factor = found.astype(jnp.float32) / (c + len_row)
                    parts.append((c * idf_ref[left * slots + i] * factor).astype(jnp.bfloat16))
                right_tile = jnp.concatenate(parts, axis=0)
                gram = jnp.dot(left_ref[left], right_tile, preferred_element_type=jnp.float32)
                for g in range(n_term):
                    out_ref[order_ref[g], k] = gram[g * part : (g + 1) * part]
            return carry

        lax.fori_loop(0, size // UNROLL, multiply, 0)

    smem = pl.BlockSpec(memory_space=pltpu.SMEM)
    vmem = pl.BlockSpec(memory_space=pltpu.VMEM)
    anywhere = pl.BlockSpec(memory_space=pl.ANY)
    return pl.pallas_call(
        kernel,
        in_specs=[smem] * 4 + [vmem] * 3 + [anywhere] * len(pieces),
        out_specs=vmem,
        out_shape=jax.ShapeDtypeStruct((n_term, size, part, rows), jnp.float32),
        scratch_shapes=[
            pltpu.VMEM((size, slots * terms, rows), jnp.bfloat16),
            pltpu.SemaphoreType.DMA((size,)),
        ],
        name="gram",
    )(select, own_ids, all_ids, order, left_tiles, idf_tiles, len_rows, *pieces)


def shards(counts, block_ids, live_slots, lengths, pairs, pair_count):
    blocks, slots, rows, terms = counts.shape
    n_doc = lax.axis_size("doc")
    n_term = lax.axis_size("term")
    doc_at = lax.axis_index("doc")
    term_at = lax.axis_index("term")
    docs_all = lengths.shape[0] * n_doc
    own_slots = blocks * slots
    tile_rows = own_slots * terms
    payload_rows = tile_rows + SMALL_ROWS

    live_counts = jnp.where(live_slots[:, :, None, None] > 0, counts, 0)
    col_docs = jnp.sum((live_counts > 0).astype(jnp.int32), axis=2).reshape(own_slots, terms)
    own_ids = block_ids.reshape(-1)
    id_row = jnp.pad(own_ids, (0, terms - own_slots)).reshape(1, terms)
    own_lengths = lengths.reshape(blocks, rows)
    small = jnp.concatenate([col_docs, split_bytes(own_lengths), split_bytes(id_row)], axis=0)
    small = jnp.pad(small, ((0, SMALL_ROWS - small.shape[0]), (0, 0)))
    tiles = jnp.swapaxes(live_counts, 2, 3).astype(jnp.bfloat16).reshape(tile_rows, rows)
    ring = gather_ring(jnp.concatenate([tiles, small.astype(jnp.bfloat16)], axis=0), 0)
    small_ring = ring.reshape(SIDE, payload_rows, rows)[:, tile_rows:]
    pieces = gather_rest(ring)
    small_all = gather_sibling(gather_ring(small_ring, 1))

    def joined(first, count):
        high = small_all[:, first : first + count].astype(jnp.float32)
        low = small_all[:, first + count : first + 2 * count].astype(jnp.float32)
        return high * BYTE + low

    col_all = small_all[:, :own_slots].reshape(n_doc * own_slots, terms)
    len_all = joined(own_slots, blocks).reshape(n_doc * blocks, rows)
    all_ids = joined(own_slots + 2 * blocks, 1)[:, 0, :own_slots].astype(jnp.int32).reshape(-1)

    same_ids = (own_ids[:, None] == all_ids[None, :]).astype(jnp.bfloat16)
    doc_freq = jnp.dot(same_ids, col_all, preferred_element_type=jnp.float32)
    inv_freq = jnp.log(1.0 + (docs_all - doc_freq + 0.5) / (doc_freq + 0.5))
    idf = inv_freq * (saturation + 1.0)
    avg_len = jnp.sum(len_all) / docs_all
    len_rows = saturation * (1.0 - length_weight + length_weight * len_all / avg_len)
    own_len = saturation * (
        1.0 - length_weight + length_weight * own_lengths.astype(jnp.float32) / avg_len
    )
    own_c = jnp.swapaxes(live_counts, 1, 2).reshape(blocks, rows, slots * terms).astype(jnp.float32)
    weight = idf.reshape(blocks, 1, slots * terms) * own_c / (own_c + own_len[:, :, None])
    square_part = jnp.sum(weight * weight, axis=2)
    square_sum = square_part
    for bit in range(1, n_term):
        square_sum = square_sum + swap_term(square_part, bit, n_term)
    norm = lax.rsqrt(square_sum + epsilon)
    left_tiles = (weight * (norm * GRAM_SCALE)[:, :, None]).astype(jnp.bfloat16)
    idf_tiles = jnp.broadcast_to(idf[:, :, None], (own_slots, terms, rows))

    left_sel = pairs[:, 0] - doc_at * blocks
    right_sel = pairs[:, 1]
    piece, spot, right_rel = place_right(right_sel, doc_at, blocks)
    start_row = spot * payload_rows + (right_sel % blocks) * (slots * terms)
    select = jnp.stack([left_sel, right_rel, piece, start_row])
    apart = jnp.arange(n_term, dtype=jnp.int32) ^ term_at
    order = (apart % 2) * 2 + apart // 2
    live = jnp.arange(pairs.shape[0], dtype=jnp.int32) < pair_count[0]
    kept = []
    ready = []
    first = 0
    for step, size in enumerate(CHUNKS):
        if step >= 2:
            select, _ = lax.optimization_barrier((select, ready[step - 2]))
        grams = gram_chunk(
            first, size, select, own_ids, all_ids, order, left_tiles, idf_tiles, len_rows, pieces
        )
        first += size
        near = swap_term(grams[2:].astype(jnp.float16), 1, n_term)
        pass_on = (grams[1] + near[1].astype(jnp.float32)).astype(jnp.float16)
        ready.append(pass_on)
        kept.append((grams[0], near[0], swap_term(pass_on, 2, n_term)))
    early, _ = lax.optimization_barrier((tuple(kept[:-1]), ready[-1]))
    totals = [
        mine + near.astype(jnp.float32) + far.astype(jnp.float32)
        for mine, near, far in (*early, kept[-1])
    ]
    norm, _ = lax.optimization_barrier((norm, ready[-2]))
    norm_ring = gather_ring(norm[None], 0)
    norm_ring, _ = lax.optimization_barrier((norm_ring, ready[-1]))
    norm_rows = gather_sibling(gather_ring(norm_ring, 1))
    norm_rows = norm_rows.reshape(n_doc * blocks, rows)
    right_norm = jnp.where(live[:, None], norm_rows[right_rel] * (1.0 / GRAM_SCALE), 0.0)
    return jnp.concatenate(totals, axis=0) * right_norm[:, None, :]


def solution(mesh):
    in_specs = (
        P("doc", "term", None, None),
        P("doc", "term"),
        P("doc", "term"),
        P("doc"),
        P(("doc", "pair"), None),
        P(("doc", "pair")),
    )
    out_specs = P(("doc", "pair"), "term", None)
    return jax.shard_map(shards, mesh=mesh, in_specs=in_specs, out_specs=out_specs, check_vma=False)
```

```python
import jax
import jax.numpy as jnp
from jax import lax
from jax.experimental import pallas as pl
from jax.experimental.pallas import tpu as pltpu
from jax.sharding import PartitionSpec as P


SIDE = 4
CORES = 2
UNROLL = 4
CHUNKS = (16, 24, 24)
GRAM_SCALE = 32.0
SMALL_ROWS = 32

saturation = 1.2
length_weight = 0.75
epsilon = 1e-06


def doc_of(y, x, core):
    return ((y % SIDE) * SIDE + x % SIDE) * CORES + core % CORES


def permute_doc(value, source):
    moves = [
        (doc_of(*source(y, x, c)), doc_of(y, x, c))
        for y in range(SIDE)
        for x in range(SIDE)
        for c in range(CORES)
    ]
    return lax.ppermute(value, "doc", moves)


def from_sibling(value):
    return permute_doc(value, lambda y, x, c: (y, x, c + 1))


def from_ring(value, phase, shift):
    def source(y, x, c):
        return (y, x + shift, c) if c == phase else (y + shift, x, c)

    return permute_doc(value, source)


def gather_ring(value, phase):
    return jnp.concatenate([value] + [from_ring(value, phase, s) for s in (1, 2, 3)], axis=0)


def gather_sibling(value):
    return jnp.concatenate([value, from_sibling(value)], axis=0)


def gather_rest(ring):
    half = ring.shape[0] // 2
    ahead = from_ring(ring, 1, 1)
    behind = from_ring(ring, 1, 3)
    across_low = from_ring(ahead[:half], 1, 1)
    across_high = from_ring(behind[half:], 1, 3)
    own = [ring, ahead, behind, across_low, across_high]
    return own + [from_sibling(piece) for piece in own]


def place_right(doc, doc_at):
    core = doc % CORES
    dx = (doc // CORES - doc_at // CORES) % SIDE
    dy = (doc // (SIDE * CORES) - doc_at // (SIDE * CORES)) % SIDE
    dcore = (doc - doc_at) % CORES
    inner = jnp.where(core == 0, dx, dy)
    outer = jnp.where(core == 0, dy, dx)
    piece = jnp.where(
        outer == 0, 0, jnp.where(outer == 1, 1, jnp.where(outer == 3, 2, 3 + inner // (SIDE // 2)))
    )
    spot = jnp.where(outer == 2, inner % (SIDE // 2), inner)
    return piece + dcore * 5, spot, (dcore * SIDE + outer) * SIDE + inner


def swap_term(value, bit, n_term):
    return lax.ppermute(value, "term", [(a, a ^ bit) for a in range(n_term)])


def prepare(counts, block_ids, live_slots, lengths):
    blocks, slots, rows, terms = counts.shape
    own_slots = blocks * slots
    tile_rows = own_slots * terms

    def kernel(ids_ref, live_ref, length_ref, count_ref, payload_ref, own_ref):
        cols = []
        id_rows = []
        for b in range(blocks):
            for s in range(slots):
                c = jnp.where(live_ref[b, s] > 0, count_ref[b, s], 0).astype(jnp.float32)
                at = (b * slots + s) * terms
                payload_ref[at : at + terms, :] = c.T.astype(jnp.bfloat16)
                own_ref[b, :, s * terms : (s + 1) * terms] = c.astype(jnp.bfloat16)
                cols.append(jnp.sum(jnp.where(c > 0.0, 1.0, 0.0), axis=0, keepdims=True))
                id_rows.append(jnp.full((1, rows), ids_ref[b, s], jnp.int32))
        ids = jnp.concatenate(id_rows, axis=0)
        length = length_ref[...]
        halves = lambda whole: ((whole >> 8).astype(jnp.float32), (whole & 255).astype(jnp.float32))
        spare = jnp.zeros((SMALL_ROWS - 3 * own_slots - 2 * blocks, rows), jnp.float32)
        small = jnp.concatenate(cols + [*halves(ids), *halves(length), spare], axis=0)
        payload_ref[tile_rows:, :] = small.astype(jnp.bfloat16)

    smem = pl.BlockSpec(memory_space=pltpu.SMEM)
    vmem = pl.BlockSpec(memory_space=pltpu.VMEM)
    return pl.pallas_call(
        kernel,
        in_specs=[smem, smem, vmem, vmem],
        out_specs=[vmem, vmem],
        out_shape=[
            jax.ShapeDtypeStruct((tile_rows + SMALL_ROWS, rows), jnp.bfloat16),
            jax.ShapeDtypeStruct((blocks, rows, slots * terms), jnp.bfloat16),
        ],
        name="prepare",
    )(block_ids, live_slots, lengths.reshape(blocks, rows), counts)


def weigh(block_ids, small_own, small_sibling, own_counts):
    blocks, rows, width = own_counts.shape
    slots = block_ids.shape[1]
    terms = width // slots
    own_slots = blocks * slots
    half_docs = small_own.shape[0]
    docs_all = 2 * half_docs * blocks * rows

    def kernel(ids_ref, near_ref, far_ref, own_ref, id_ref, length_ref, idf_ref, weight_ref, square_ref):
        small = jnp.concatenate([near_ref[...], far_ref[...]], axis=0).astype(jnp.float32)
        cols = small[:, :own_slots]
        ids = small[:, own_slots : 2 * own_slots] * 256.0 + small[:, 2 * own_slots : 3 * own_slots]
        ids = ids.astype(jnp.int32)
        id_ref[...] = ids
        packed = small[:, 3 * own_slots :]
        length = packed * 256.0 + pltpu.roll(packed, packed.shape[1] - blocks, 1)
        row_at = lax.broadcasted_iota(jnp.int32, length.shape, 1)
        total = jnp.sum(jnp.sum(jnp.where(row_at < blocks, length, 0.0), axis=0), keepdims=True)
        avg_len = total / docs_all
        scaled = saturation * (1.0 - length_weight + length_weight * length / avg_len[None])
        length_ref[...] = scaled
        for b in range(blocks):
            own_len = jnp.broadcast_to(scaled[0, b : b + 1, :], (rows, rows)).T
            square = jnp.zeros((rows, terms), jnp.float32)
            for s in range(slots):
                here = jnp.where(ids == ids_ref[b, s], cols, 0.0)
                doc_freq = jnp.sum(jnp.sum(here, axis=0), axis=0, keepdims=True)
                inv_freq = jnp.log(1.0 + (docs_all - doc_freq + 0.5) / (doc_freq + 0.5))
                idf = inv_freq * (saturation + 1.0)
                idf_ref[b * slots + s] = jnp.broadcast_to(idf, (rows, terms)).T
                c = own_ref[b, :, s * terms : (s + 1) * terms].astype(jnp.float32)
                weight = idf * c / (c + own_len)
                weight_ref[b, :, s * terms : (s + 1) * terms] = weight
                square = square + weight * weight
            square_ref[b : b + 1, :] = jnp.sum(square.T, axis=0, keepdims=True)

    smem = pl.BlockSpec(memory_space=pltpu.SMEM)
    vmem = pl.BlockSpec(memory_space=pltpu.VMEM)
    return pl.pallas_call(
        kernel,
        in_specs=[smem, vmem, vmem, vmem],
        out_specs=[vmem] * 5,
        out_shape=[
            jax.ShapeDtypeStruct((2 * half_docs, own_slots, rows), jnp.int32),
            jax.ShapeDtypeStruct((2 * half_docs, SMALL_ROWS - 3 * own_slots, rows), jnp.float32),
            jax.ShapeDtypeStruct((own_slots, terms, rows), jnp.float32),
            jax.ShapeDtypeStruct((blocks, rows, width), jnp.float32),
            jax.ShapeDtypeStruct((blocks, rows), jnp.float32),
        ],
        name="weigh",
    )(block_ids, small_own, small_sibling, own_counts)


def gram_chunk(first, size, select, own_ids, all_ids, order, weight, squares, idf_tiles, len_rows, pieces):
    own_slots, terms, rows = idf_tiles.shape
    blocks = weight.shape[0]
    slots = own_slots // blocks
    n_term = order.shape[0]
    part = rows // n_term
    groups = size // UNROLL

    def kernel(sel_ref, own_ref, ids_ref, order_ref, *refs):
        square_refs = refs[:n_term]
        weight_hbm, idf_hbm, length_hbm = refs[n_term : n_term + 3]
        piece_refs = refs[n_term + 3 : n_term + 3 + len(pieces)]
        out_hbm, *scratch = refs[n_term + 3 + len(pieces) :]
        weight_ref, idf_ref, length_ref, left_ref, tile_buf, gram_ref, loaded, arrived, written = scratch
        loads = [
            pltpu.make_async_copy(src, dst, loaded.at[n])
            for n, (src, dst) in enumerate(
                [(weight_hbm, weight_ref), (idf_hbm, idf_ref), (length_hbm, length_ref)]
            )
        ]
        for load in loads:
            load.start()

        def fetch(k, carry):
            piece = sel_ref[3, first + k]
            spot = pl.multiple_of(sel_ref[4, first + k], SMALL_ROWS)
            for p, ref in enumerate(piece_refs):

                @pl.when(piece == p)
                def _():
                    pltpu.make_async_copy(
                        ref.at[pl.ds(spot, slots * terms)], tile_buf.at[k], arrived.at[k]
                    ).start()

            return carry

        lax.fori_loop(0, size, fetch, 0)
        square_sum = square_refs[0][...]
        for ref in square_refs[1:]:
            square_sum = square_sum + ref[...]
        norm = lax.rsqrt(square_sum + epsilon) * GRAM_SCALE
        for load in loads:
            load.wait()
        for b in range(blocks):
            column = jnp.broadcast_to(norm[b : b + 1, :], (rows, rows)).T
            for s in range(slots):
                at = slice(s * terms, (s + 1) * terms)
                left_ref[b, :, at] = (weight_ref[b, :, at] * column).astype(jnp.bfloat16)

        def multiply(step, carry):
            for p in range(UNROLL):
                k = step * UNROLL + p
                pltpu.make_async_copy(
                    piece_refs[0].at[pl.ds(0, slots * terms)], tile_buf.at[k], arrived.at[k]
                ).wait()
            for p in range(UNROLL):
                k = step * UNROLL + p
                left = sel_ref[0, first + k]
                right_doc = sel_ref[1, first + k]
                right_block = sel_ref[2, first + k]
                len_row = length_ref[right_doc, pl.ds(right_block, 1), :]
                parts = []
                for i in range(slots):
                    wanted = own_ref[left, i]
                    found = jnp.int32(0)
                    place = jnp.int32(0)
                    for j in range(slots):
                        same = ids_ref[right_doc * own_slots + right_block * slots + j] == wanted
                        found = jnp.where(same, 1, found)
                        place = jnp.where(same, j, place)
                    start = pl.multiple_of(place * terms, terms)
                    c = tile_buf[k, pl.ds(start, terms), :].astype(jnp.float32)
                    factor = found.astype(jnp.float32) / (c + len_row)
                    parts.append((c * idf_ref[left * slots + i] * factor).astype(jnp.bfloat16))
                right_tile = jnp.concatenate(parts, axis=0)
                gram = jnp.dot(left_ref[left], right_tile, preferred_element_type=jnp.float32)
                for g in range(n_term):
                    gram_ref[order_ref[g], k] = gram[g * part : (g + 1) * part]
            span = pl.ds(step * UNROLL, UNROLL)
            pltpu.make_async_copy(
                gram_ref.at[:, span], out_hbm.at[:, span], written.at[step]
            ).start()
            return carry

        lax.fori_loop(0, groups, multiply, 0)

        def drain(step, carry):
            span = pl.ds(step * UNROLL, UNROLL)
            pltpu.make_async_copy(
                gram_ref.at[:, span], out_hbm.at[:, span], written.at[step]
            ).wait()
            return carry

        lax.fori_loop(0, groups, drain, 0)

    smem = pl.BlockSpec(memory_space=pltpu.SMEM)
    vmem = pl.BlockSpec(memory_space=pltpu.VMEM)
    anywhere = pl.BlockSpec(memory_space=pl.ANY)
    return pl.pallas_call(
        kernel,
        in_specs=[smem] * 4 + [vmem] * n_term + [anywhere] * (3 + len(pieces)),
        out_specs=anywhere,
        out_shape=jax.ShapeDtypeStruct((n_term, size, part, rows), jnp.float32),
        scratch_shapes=[
            pltpu.VMEM(weight.shape, jnp.float32),
            pltpu.VMEM(idf_tiles.shape, jnp.float32),
            pltpu.VMEM(len_rows.shape, jnp.float32),
            pltpu.VMEM(weight.shape, jnp.bfloat16),
            pltpu.VMEM((size, slots * terms, rows), jnp.bfloat16),
            pltpu.VMEM((n_term, size, part, rows), jnp.float32),
            pltpu.SemaphoreType.DMA((3,)),
            pltpu.SemaphoreType.DMA((size,)),
            pltpu.SemaphoreType.DMA((groups,)),
        ],
        name="gram",
    )(select, own_ids, all_ids, order, *squares, weight, idf_tiles, len_rows, *pieces)


def whole(counts, block_ids, live_slots, lengths, pairs, pair_count):
    blocks, slots, rows, terms = counts.shape
    n_doc = lax.axis_size("doc")
    n_term = lax.axis_size("term")
    doc_at = lax.axis_index("doc")
    term_at = lax.axis_index("term")
    tile_rows = blocks * slots * terms
    payload_rows = tile_rows + SMALL_ROWS

    payload, own_counts = prepare(counts, block_ids, live_slots, lengths)
    ring = gather_ring(payload, 0)
    small_own = gather_ring(ring.reshape(SIDE, payload_rows, rows)[:, tile_rows:], 1)
    small_sibling = from_sibling(small_own)
    pieces = gather_rest(ring)
    all_ids, len_rows, idf_tiles, weight, square_part = weigh(
        block_ids, small_own, small_sibling, own_counts
    )
    all_ids = all_ids[:, :, 0].reshape(-1)
    squares = [square_part] + [swap_term(square_part, bit, n_term) for bit in range(1, n_term)]

    left_sel = pairs[:, 0] - doc_at * blocks
    right_sel = pairs[:, 1]
    piece, spot, right_doc = place_right(right_sel // blocks, doc_at)
    right_block = right_sel % blocks
    start_row = spot * payload_rows + right_block * (slots * terms)
    select = jnp.stack([left_sel, right_doc, right_block, piece, start_row])
    apart = jnp.arange(n_term, dtype=jnp.int32) ^ term_at
    order = (apart % 2) * 2 + apart // 2
    live = jnp.arange(pairs.shape[0], dtype=jnp.int32) < pair_count[0]
    kept = []
    ready = []
    first = 0
    for step, size in enumerate(CHUNKS):
        if step >= 2:
            select, _ = lax.optimization_barrier((select, ready[step - 2]))
        grams = gram_chunk(
            first, size, select, block_ids, all_ids, order, weight, squares, idf_tiles, len_rows, pieces
        )
        first += size
        near = swap_term(grams[2:].astype(jnp.float16), 1, n_term)
        pass_on = (grams[1] + near[1].astype(jnp.float32)).astype(jnp.float16)
        ready.append(pass_on)
        far = swap_term(pass_on, 2, n_term)
        kept.append((grams[0], near[0], far))
    early, _ = lax.optimization_barrier((tuple(kept[:-1]), ready[-1]))
    totals = [
        mine + near.astype(jnp.float32) + far.astype(jnp.float32)
        for mine, near, far in (*early, kept[-1])
    ]
    norm, _ = lax.optimization_barrier((lax.rsqrt(sum(squares) + epsilon), ready[-2]))
    norm_ring = gather_ring(norm[None], 0)
    norm_ring, _ = lax.optimization_barrier((norm_ring, ready[-1]))
    norm_rows = gather_sibling(gather_ring(norm_ring, 1))
    norm_rows = norm_rows.reshape(n_doc * blocks, rows)[right_doc * blocks + right_block]
    right_norm = jnp.where(live[:, None], norm_rows * (1.0 / GRAM_SCALE), 0.0)
    return jnp.concatenate(totals, axis=0) * right_norm[:, None, :]


def solution(mesh):
    in_specs = (
        P("doc", "term", None, None),
        P("doc", "term"),
        P("doc", "term"),
        P("doc"),
        P(("doc", "pair"), None),
        P(("doc", "pair")),
    )
    out_specs = P(("doc", "pair"), "term", None)
    return jax.shard_map(whole, mesh=mesh, in_specs=in_specs, out_specs=out_specs, check_vma=False)
```

```python
import jax
import jax.numpy as jnp
from jax import lax
from jax.experimental import pallas as pl
from jax.experimental.pallas import tpu as pltpu
from jax.sharding import PartitionSpec as P


SIDE = 4
CORES = 2
UNROLL = 4
CHUNKS = (16, 24, 24)
GRAM_SCALE = 32.0
SMALL_ROWS = 32

saturation = 1.2
length_weight = 0.75
epsilon = 1e-06


def doc_of(y, x, core):
    return ((y % SIDE) * SIDE + x % SIDE) * CORES + core % CORES


def permute_doc(value, source):
    moves = [
        (doc_of(*source(y, x, c)), doc_of(y, x, c))
        for y in range(SIDE)
        for x in range(SIDE)
        for c in range(CORES)
    ]
    return lax.ppermute(value, "doc", moves)


def from_sibling(value):
    return permute_doc(value, lambda y, x, c: (y, x, c + 1))


def from_ring(value, phase, shift):
    def source(y, x, c):
        return (y, x + shift, c) if c == phase else (y + shift, x, c)

    return permute_doc(value, source)


def gather_ring(value, phase):
    return jnp.concatenate([value] + [from_ring(value, phase, s) for s in (1, 2, 3)], axis=0)


def gather_sibling(value):
    return jnp.concatenate([value, from_sibling(value)], axis=0)


def gather_rest(low, high):
    ahead_low = from_ring(low, 1, 1)
    behind_high = from_ring(high, 1, 3)
    ahead_high = from_ring(high, 1, 1)
    behind_low = from_ring(low, 1, 3)
    across_low = from_ring(ahead_low, 1, 1)
    across_high = from_ring(behind_high, 1, 3)
    early = [low, high]
    late = [ahead_low, ahead_high, across_low, across_high, behind_low, behind_high]
    early_far = [from_sibling(piece) for piece in early]
    late_far = [from_sibling(piece) for piece in late]
    return early + late + early_far + late_far


def place_right(doc, doc_at):
    core = doc % CORES
    dx = (doc // CORES - doc_at // CORES) % SIDE
    dy = (doc // (SIDE * CORES) - doc_at // (SIDE * CORES)) % SIDE
    dcore = (doc - doc_at) % CORES
    inner = jnp.where(core == 0, dx, dy)
    outer = jnp.where(core == 0, dy, dx)
    piece = (dcore * SIDE + outer) * 2 + inner // 2
    return piece, inner % 2, (dcore * SIDE + outer) * SIDE + inner


def swap_term(value, bit, n_term):
    return lax.ppermute(value, "term", [(a, a ^ bit) for a in range(n_term)])


def prepare(counts, block_ids, live_slots, lengths):
    blocks, slots, rows, terms = counts.shape
    own_slots = blocks * slots
    tile_rows = own_slots * terms

    def kernel(ids_ref, live_ref, length_ref, count_ref, payload_ref, own_ref):
        cols = []
        id_rows = []
        for b in range(blocks):
            for s in range(slots):
                c = jnp.where(live_ref[b, s] > 0, count_ref[b, s], 0).astype(jnp.float32)
                at = (b * slots + s) * terms
                payload_ref[at : at + terms, :] = c.T.astype(jnp.bfloat16)
                own_ref[b, :, s * terms : (s + 1) * terms] = c.astype(jnp.bfloat16)
                cols.append(jnp.sum(jnp.where(c > 0.0, 1.0, 0.0), axis=0, keepdims=True))
                id_rows.append(jnp.full((1, rows), ids_ref[b, s], jnp.int32))
        ids = jnp.concatenate(id_rows, axis=0)
        length = length_ref[...]
        halves = lambda whole: ((whole >> 8).astype(jnp.float32), (whole & 255).astype(jnp.float32))
        spare = jnp.zeros((SMALL_ROWS - 3 * own_slots - 2 * blocks, rows), jnp.float32)
        small = jnp.concatenate(cols + [*halves(ids), *halves(length), spare], axis=0)
        payload_ref[tile_rows:, :] = small.astype(jnp.bfloat16)

    smem = pl.BlockSpec(memory_space=pltpu.SMEM)
    vmem = pl.BlockSpec(memory_space=pltpu.VMEM)
    return pl.pallas_call(
        kernel,
        in_specs=[smem, smem, vmem, vmem],
        out_specs=[vmem, vmem],
        out_shape=[
            jax.ShapeDtypeStruct((tile_rows + SMALL_ROWS, rows), jnp.bfloat16),
            jax.ShapeDtypeStruct((blocks, rows, slots * terms), jnp.bfloat16),
        ],
        name="prepare",
    )(block_ids, live_slots, lengths.reshape(blocks, rows), counts)


def weigh(block_ids, small_own, small_sibling, own_counts):
    blocks, rows, width = own_counts.shape
    slots = block_ids.shape[1]
    terms = width // slots
    own_slots = blocks * slots
    half_docs = small_own.shape[0]
    docs_all = 2 * half_docs * blocks * rows

    def kernel(ids_ref, near_ref, far_ref, own_ref, id_ref, length_ref, idf_ref, weight_ref, square_ref):
        small = jnp.concatenate([near_ref[...], far_ref[...]], axis=0).astype(jnp.float32)
        cols = small[:, :own_slots]
        ids = small[:, own_slots : 2 * own_slots] * 256.0 + small[:, 2 * own_slots : 3 * own_slots]
        ids = ids.astype(jnp.int32)
        id_ref[...] = ids
        packed = small[:, 3 * own_slots :]
        length = packed * 256.0 + pltpu.roll(packed, packed.shape[1] - blocks, 1)
        row_at = lax.broadcasted_iota(jnp.int32, length.shape, 1)
        total = jnp.sum(jnp.sum(jnp.where(row_at < blocks, length, 0.0), axis=0), keepdims=True)
        avg_len = total / docs_all
        scaled = saturation * (1.0 - length_weight + length_weight * length / avg_len[None])
        length_ref[...] = scaled
        for b in range(blocks):
            own_len = jnp.broadcast_to(scaled[0, b : b + 1, :], (rows, rows)).T
            square = jnp.zeros((rows, terms), jnp.float32)
            for s in range(slots):
                here = jnp.where(ids == ids_ref[b, s], cols, 0.0)
                doc_freq = jnp.sum(jnp.sum(here, axis=0), axis=0, keepdims=True)
                inv_freq = jnp.log(1.0 + (docs_all - doc_freq + 0.5) / (doc_freq + 0.5))
                idf = inv_freq * (saturation + 1.0)
                idf_ref[b * slots + s] = jnp.broadcast_to(idf, (rows, terms)).T
                c = own_ref[b, :, s * terms : (s + 1) * terms].astype(jnp.float32)
                weight = idf * c / (c + own_len)
                weight_ref[b, :, s * terms : (s + 1) * terms] = weight
                square = square + weight * weight
            square_ref[b : b + 1, :] = jnp.sum(square.T, axis=0, keepdims=True)

    smem = pl.BlockSpec(memory_space=pltpu.SMEM)
    vmem = pl.BlockSpec(memory_space=pltpu.VMEM)
    return pl.pallas_call(
        kernel,
        in_specs=[smem, vmem, vmem, vmem],
        out_specs=[vmem] * 5,
        out_shape=[
            jax.ShapeDtypeStruct((2 * half_docs, own_slots, rows), jnp.int32),
            jax.ShapeDtypeStruct((2 * half_docs, SMALL_ROWS - 3 * own_slots, rows), jnp.float32),
            jax.ShapeDtypeStruct((own_slots, terms, rows), jnp.float32),
            jax.ShapeDtypeStruct((blocks, rows, width), jnp.float32),
            jax.ShapeDtypeStruct((blocks, rows), jnp.float32),
        ],
        name="weigh",
    )(block_ids, small_own, small_sibling, own_counts)


def gram_chunk(first, size, select, own_ids, all_ids, order, weight, squares, idf_tiles, len_rows, pieces):
    own_slots, terms, rows = idf_tiles.shape
    blocks = weight.shape[0]
    slots = own_slots // blocks
    n_term = order.shape[0]
    part = rows // n_term
    groups = size // UNROLL

    def kernel(sel_ref, own_ref, ids_ref, order_ref, *refs):
        square_refs = refs[:n_term]
        weight_hbm, idf_hbm, length_hbm = refs[n_term : n_term + 3]
        piece_refs = refs[n_term + 3 : n_term + 3 + len(pieces)]
        out_hbm, *scratch = refs[n_term + 3 + len(pieces) :]
        weight_ref, idf_ref, length_ref, left_ref, tile_buf, gram_ref, loaded, arrived, written = scratch
        loads = [
            pltpu.make_async_copy(src, dst, loaded.at[n])
            for n, (src, dst) in enumerate(
                [(weight_hbm, weight_ref), (idf_hbm, idf_ref), (length_hbm, length_ref)]
            )
        ]
        for load in loads:
            load.start()

        def fetch(k, carry):
            piece = sel_ref[3, first + k]
            spot = pl.multiple_of(sel_ref[4, first + k], SMALL_ROWS)
            for quad in range(len(pieces) // 4):

                @pl.when(piece // 4 == quad)
                def _():
                    for p in range(4 * quad, 4 * quad + 4):

                        @pl.when(piece == p)
                        def _():
                            pltpu.make_async_copy(
                                piece_refs[p].at[pl.ds(spot, slots * terms)],
                                tile_buf.at[k],
                                arrived.at[k],
                            ).start()

            return carry

        lax.fori_loop(0, size, fetch, 0)
        square_sum = square_refs[0][...]
        for ref in square_refs[1:]:
            square_sum = square_sum + ref[...]
        norm = lax.rsqrt(square_sum + epsilon) * GRAM_SCALE
        for load in loads:
            load.wait()
        for b in range(blocks):
            column = jnp.broadcast_to(norm[b : b + 1, :], (rows, rows)).T
            for s in range(slots):
                at = slice(s * terms, (s + 1) * terms)
                left_ref[b, :, at] = (weight_ref[b, :, at] * column).astype(jnp.bfloat16)

        def multiply(step, carry):
            for p in range(UNROLL):
                k = step * UNROLL + p
                pltpu.make_async_copy(
                    piece_refs[0].at[pl.ds(0, slots * terms)], tile_buf.at[k], arrived.at[k]
                ).wait()
            for p in range(UNROLL):
                k = step * UNROLL + p
                left = sel_ref[0, first + k]
                right_doc = sel_ref[1, first + k]
                right_block = sel_ref[2, first + k]
                len_row = length_ref[right_doc, pl.ds(right_block, 1), :]
                parts = []
                for i in range(slots):
                    wanted = own_ref[left, i]
                    found = jnp.int32(0)
                    place = jnp.int32(0)
                    for j in range(slots):
                        same = ids_ref[right_doc * own_slots + right_block * slots + j] == wanted
                        found = jnp.where(same, 1, found)
                        place = jnp.where(same, j, place)
                    start = pl.multiple_of(place * terms, terms)
                    c = tile_buf[k, pl.ds(start, terms), :].astype(jnp.float32)
                    factor = found.astype(jnp.float32) / (c + len_row)
                    parts.append((c * idf_ref[left * slots + i] * factor).astype(jnp.bfloat16))
                right_tile = jnp.concatenate(parts, axis=0)
                gram = jnp.dot(left_ref[left], right_tile, preferred_element_type=jnp.float32)
                for g in range(n_term):
                    gram_ref[order_ref[g], k] = gram[g * part : (g + 1) * part]
            span = pl.ds(step * UNROLL, UNROLL)
            pltpu.make_async_copy(
                gram_ref.at[:, span], out_hbm.at[:, span], written.at[step]
            ).start()
            return carry

        lax.fori_loop(0, groups, multiply, 0)

        def drain(step, carry):
            span = pl.ds(step * UNROLL, UNROLL)
            pltpu.make_async_copy(
                gram_ref.at[:, span], out_hbm.at[:, span], written.at[step]
            ).wait()
            return carry

        lax.fori_loop(0, groups, drain, 0)

    smem = pl.BlockSpec(memory_space=pltpu.SMEM)
    vmem = pl.BlockSpec(memory_space=pltpu.VMEM)
    anywhere = pl.BlockSpec(memory_space=pl.ANY)
    return pl.pallas_call(
        kernel,
        in_specs=[smem] * 4 + [vmem] * n_term + [anywhere] * (3 + len(pieces)),
        out_specs=anywhere,
        out_shape=jax.ShapeDtypeStruct((n_term, size, part, rows), jnp.float32),
        scratch_shapes=[
            pltpu.VMEM(weight.shape, jnp.float32),
            pltpu.VMEM(idf_tiles.shape, jnp.float32),
            pltpu.VMEM(len_rows.shape, jnp.float32),
            pltpu.VMEM(weight.shape, jnp.bfloat16),
            pltpu.VMEM((size, slots * terms, rows), jnp.bfloat16),
            pltpu.VMEM((n_term, size, part, rows), jnp.float32),
            pltpu.SemaphoreType.DMA((3,)),
            pltpu.SemaphoreType.DMA((size,)),
            pltpu.SemaphoreType.DMA((groups,)),
        ],
        name="gram",
    )(select, own_ids, all_ids, order, *squares, weight, idf_tiles, len_rows, *pieces)


def whole(counts, block_ids, live_slots, lengths, pairs, pair_count):
    blocks, slots, rows, terms = counts.shape
    n_doc = lax.axis_size("doc")
    n_term = lax.axis_size("term")
    doc_at = lax.axis_index("doc")
    term_at = lax.axis_index("term")
    tile_rows = blocks * slots * terms
    payload_rows = tile_rows + SMALL_ROWS

    payload, own_counts = prepare(counts, block_ids, live_slots, lengths)
    ring = [payload] + [from_ring(payload, 0, s) for s in (1, 2, 3)]
    low = jnp.concatenate(ring[:2], axis=0)
    high = jnp.concatenate(ring[2:], axis=0)
    small_ring = jnp.stack([piece[tile_rows:] for piece in ring])
    small_own = gather_ring(small_ring, 1)
    small_sibling = from_sibling(small_own)
    pieces = gather_rest(low, high)
    all_ids, len_rows, idf_tiles, weight, square_part = weigh(
        block_ids, small_own, small_sibling, own_counts
    )
    all_ids = all_ids[:, :, 0].reshape(-1)
    squares = [square_part] + [swap_term(square_part, bit, n_term) for bit in range(1, n_term)]

    left_sel = pairs[:, 0] - doc_at * blocks
    right_sel = pairs[:, 1]
    piece, spot, right_doc = place_right(right_sel // blocks, doc_at)
    right_block = right_sel % blocks
    start_row = spot * payload_rows + right_block * (slots * terms)
    select = jnp.stack([left_sel, right_doc, right_block, piece, start_row])
    apart = jnp.arange(n_term, dtype=jnp.int32) ^ term_at
    order = (apart % 2) * 2 + apart // 2
    live = jnp.arange(pairs.shape[0], dtype=jnp.int32) < pair_count[0]
    kept = []
    ready = []
    first = 0
    for step, size in enumerate(CHUNKS):
        if step >= 2:
            select, _ = lax.optimization_barrier((select, ready[step - 2]))
        grams = gram_chunk(
            first, size, select, block_ids, all_ids, order, weight, squares, idf_tiles, len_rows, pieces
        )
        first += size
        near = swap_term(grams[2:].astype(jnp.float16), 1, n_term)
        pass_on = (grams[1] + near[1].astype(jnp.float32)).astype(jnp.float16)
        ready.append(pass_on)
        far = swap_term(pass_on, 2, n_term)
        kept.append((grams[0], near[0], far))
    early, _ = lax.optimization_barrier((tuple(kept[:-1]), ready[-1]))
    totals = [
        mine + near.astype(jnp.float32) + far.astype(jnp.float32)
        for mine, near, far in (*early, kept[-1])
    ]
    norm, _ = lax.optimization_barrier((lax.rsqrt(sum(squares) + epsilon), ready[-2]))
    norm_ring = gather_ring(norm[None], 0)
    norm_ring, _ = lax.optimization_barrier((norm_ring, ready[-1]))
    norm_rows = gather_sibling(gather_ring(norm_ring, 1))
    norm_rows = norm_rows.reshape(n_doc * blocks, rows)[right_doc * blocks + right_block]
    right_norm = jnp.where(live[:, None], norm_rows * (1.0 / GRAM_SCALE), 0.0)
    return jnp.concatenate(totals, axis=0) * right_norm[:, None, :]


def solution(mesh):
    in_specs = (
        P("doc", "term", None, None),
        P("doc", "term"),
        P("doc", "term"),
        P("doc"),
        P(("doc", "pair"), None),
        P(("doc", "pair")),
    )
    out_specs = P(("doc", "pair"), "term", None)
    return jax.shard_map(whole, mesh=mesh, in_specs=in_specs, out_specs=out_specs, check_vma=False)
```

```python
import jax
import jax.numpy as jnp
from jax import lax
from jax.experimental import pallas as pl
from jax.experimental.pallas import tpu as pltpu
from jax.sharding import PartitionSpec as P


SIDE = 4
CORES = 2
UNROLL = 4
CHUNKS = (24, 24, 16)
GRAM_SCALE = 32.0
SMALL_ROWS = 32

saturation = 1.2
length_weight = 0.75
epsilon = 1e-06


def doc_of(y, x, core):
    return ((y % SIDE) * SIDE + x % SIDE) * CORES + core % CORES


def permute_doc(value, source):
    moves = [
        (doc_of(*source(y, x, c)), doc_of(y, x, c))
        for y in range(SIDE)
        for x in range(SIDE)
        for c in range(CORES)
    ]
    return lax.ppermute(value, "doc", moves)


def from_sibling(value):
    return permute_doc(value, lambda y, x, c: (y, x, c + 1))


def from_ring(value, phase, shift):
    def source(y, x, c):
        return (y, x + shift, c) if c == phase else (y + shift, x, c)

    return permute_doc(value, source)


def gather_ring(value, phase):
    return jnp.concatenate([value] + [from_ring(value, phase, s) for s in (1, 2, 3)], axis=0)


def gather_sibling(value):
    return jnp.concatenate([value, from_sibling(value)], axis=0)


def gather_rest(low, high):
    ahead_low = from_ring(low, 1, 1)
    behind_high = from_ring(high, 1, 3)
    ahead_high = from_ring(high, 1, 1)
    behind_low = from_ring(low, 1, 3)
    across_low = from_ring(ahead_low, 1, 1)
    across_high = from_ring(behind_high, 1, 3)
    early = [low, high]
    late = [ahead_low, ahead_high, across_low, across_high, behind_low, behind_high]
    early_far = [from_sibling(piece) for piece in early]
    late_far = [from_sibling(piece) for piece in late]
    return early + late + early_far + late_far


def place_right(doc, doc_at):
    core = doc % CORES
    dx = (doc // CORES - doc_at // CORES) % SIDE
    dy = (doc // (SIDE * CORES) - doc_at // (SIDE * CORES)) % SIDE
    dcore = (doc - doc_at) % CORES
    inner = jnp.where(core == 0, dx, dy)
    outer = jnp.where(core == 0, dy, dx)
    piece = (dcore * SIDE + outer) * 2 + inner // 2
    return piece, inner % 2, (dcore * SIDE + outer) * SIDE + inner


def place_owner(owner, term_at):
    apart = owner ^ term_at
    return (apart % 2) * 2 + apart // 2


def swap_term(value, bit, n_term):
    return lax.ppermute(value, "term", [(a, a ^ bit) for a in range(n_term)])


def prepare(counts, block_ids, live_slots, lengths):
    blocks, slots, rows, terms = counts.shape
    own_slots = blocks * slots
    tile_rows = own_slots * terms

    def kernel(ids_ref, live_ref, length_ref, count_ref, payload_ref, own_ref):
        cols = []
        id_rows = []
        for b in range(blocks):
            for s in range(slots):
                c = jnp.where(live_ref[b, s] > 0, count_ref[b, s], 0).astype(jnp.float32)
                at = (b * slots + s) * terms
                payload_ref[at : at + terms, :] = c.T.astype(jnp.bfloat16)
                own_ref[b, :, s * terms : (s + 1) * terms] = c.astype(jnp.bfloat16)
                cols.append(jnp.sum(jnp.where(c > 0.0, 1.0, 0.0), axis=0, keepdims=True))
                id_rows.append(jnp.full((1, rows), ids_ref[b, s], jnp.int32))
        ids = jnp.concatenate(id_rows, axis=0)
        length = length_ref[...]
        halves = lambda whole: ((whole >> 8).astype(jnp.float32), (whole & 255).astype(jnp.float32))
        spare = jnp.zeros((SMALL_ROWS - 3 * own_slots - 2 * blocks, rows), jnp.float32)
        small = jnp.concatenate(cols + [*halves(ids), *halves(length), spare], axis=0)
        payload_ref[tile_rows:, :] = small.astype(jnp.bfloat16)

    smem = pl.BlockSpec(memory_space=pltpu.SMEM)
    vmem = pl.BlockSpec(memory_space=pltpu.VMEM)
    return pl.pallas_call(
        kernel,
        in_specs=[smem, smem, vmem, vmem],
        out_specs=[vmem, vmem],
        out_shape=[
            jax.ShapeDtypeStruct((tile_rows + SMALL_ROWS, rows), jnp.bfloat16),
            jax.ShapeDtypeStruct((blocks, rows, slots * terms), jnp.bfloat16),
        ],
        name="prepare",
    )(block_ids, live_slots, lengths.reshape(blocks, rows), counts)


def weigh(block_ids, small_parts, own_counts):
    blocks, rows, width = own_counts.shape
    slots = block_ids.shape[1]
    terms = width // slots
    own_slots = blocks * slots
    n_doc = len(small_parts) * small_parts[0].shape[0]
    docs_all = n_doc * blocks * rows

    def kernel(ids_ref, own_ref, *refs):
        small_refs = refs[: len(small_parts)]
        id_ref, length_ref, idf_ref, weight_ref, square_ref = refs[len(small_parts) :]
        small = jnp.concatenate([ref[...].astype(jnp.float32) for ref in small_refs], axis=0)
        cols = small[:, :own_slots]
        ids = small[:, own_slots : 2 * own_slots] * 256.0 + small[:, 2 * own_slots : 3 * own_slots]
        flat = ids.reshape(n_doc * own_slots, rows)
        for h in range(n_doc * own_slots // rows):
            turned = flat[h * rows : (h + 1) * rows].T
            id_ref[h : h + 1, :] = turned[:1].astype(jnp.int32)
        ids = ids.astype(jnp.int32)
        packed = small[:, 3 * own_slots :]
        length = packed * 256.0 + pltpu.roll(packed, packed.shape[1] - blocks, 1)
        row_at = lax.broadcasted_iota(jnp.int32, length.shape, 1)
        total = jnp.sum(jnp.sum(jnp.where(row_at < blocks, length, 0.0), axis=0), keepdims=True)
        avg_len = total / docs_all
        scaled = saturation * (1.0 - length_weight + length_weight * length / avg_len[None])
        length_ref[...] = scaled
        for b in range(blocks):
            own_len = jnp.broadcast_to(scaled[0, b : b + 1, :], (rows, rows)).T
            square = jnp.zeros((rows, terms), jnp.float32)
            for s in range(slots):
                here = jnp.where(ids == ids_ref[b, s], cols, 0.0)
                doc_freq = jnp.sum(jnp.sum(here, axis=0), axis=0, keepdims=True)
                inv_freq = jnp.log(1.0 + (docs_all - doc_freq + 0.5) / (doc_freq + 0.5))
                idf = inv_freq * (saturation + 1.0)
                idf_ref[b * slots + s] = jnp.broadcast_to(idf, (rows, terms)).T
                c = own_ref[b, :, s * terms : (s + 1) * terms].astype(jnp.float32)
                weight = idf * c / (c + own_len)
                weight_ref[b, :, s * terms : (s + 1) * terms] = weight
                square = square + weight * weight
            square_ref[b : b + 1, :] = jnp.sum(square.T, axis=0, keepdims=True)

    smem = pl.BlockSpec(memory_space=pltpu.SMEM)
    vmem = pl.BlockSpec(memory_space=pltpu.VMEM)
    return pl.pallas_call(
        kernel,
        in_specs=[smem, vmem] + [vmem] * len(small_parts),
        out_specs=[vmem] * 5,
        out_shape=[
            jax.ShapeDtypeStruct((n_doc * own_slots // rows, rows), jnp.int32),
            jax.ShapeDtypeStruct((n_doc, SMALL_ROWS - 3 * own_slots, rows), jnp.float32),
            jax.ShapeDtypeStruct((own_slots, terms, rows), jnp.float32),
            jax.ShapeDtypeStruct((blocks, rows, width), jnp.float32),
            jax.ShapeDtypeStruct((blocks, rows), jnp.float32),
        ],
        name="weigh",
    )(block_ids, own_counts, *small_parts)


def gram_chunk(first, size, pairs, own_ids, all_ids, weight, squares, idf_tiles, len_rows, pieces):
    own_slots, terms, rows = idf_tiles.shape
    blocks = weight.shape[0]
    slots = own_slots // blocks
    n_term = len(squares)
    part = rows // n_term
    groups = size // UNROLL
    payload_rows = pieces[0].shape[0] // 2

    def kernel(pair_ref, own_ref, ids_ref, *refs):
        doc_at = lax.axis_index("doc")
        term_at = lax.axis_index("term")
        square_refs = refs[:n_term]
        weight_hbm, idf_hbm, length_hbm = refs[n_term : n_term + 3]
        piece_refs = refs[n_term + 3 : n_term + 3 + len(pieces)]
        out_hbm, *scratch = refs[n_term + 3 + len(pieces) :]
        weight_ref, idf_ref, length_ref, left_ref, tile_buf, gram_ref, loaded, arrived, written = scratch
        loads = [
            pltpu.make_async_copy(src, dst, loaded.at[n])
            for n, (src, dst) in enumerate(
                [(weight_hbm, weight_ref), (idf_hbm, idf_ref), (length_hbm, length_ref)]
            )
        ]
        for load in loads:
            load.start()

        def fetch(k, carry):
            right = pair_ref[first + k, 1]
            piece, spot, _ = place_right(right // blocks, doc_at)
            spot = spot * payload_rows + (right % blocks) * (slots * terms)
            spot = pl.multiple_of(spot, SMALL_ROWS)
            for quad in range(len(pieces) // 4):

                @pl.when(piece // 4 == quad)
                def _():
                    for p in range(4 * quad, 4 * quad + 4):

                        @pl.when(piece == p)
                        def _():
                            pltpu.make_async_copy(
                                piece_refs[p].at[pl.ds(spot, slots * terms)],
                                tile_buf.at[k],
                                arrived.at[k],
                            ).start()

            return carry

        lax.fori_loop(0, size, fetch, 0)
        square_sum = square_refs[0][...]
        for ref in square_refs[1:]:
            square_sum = square_sum + ref[...]
        norm = lax.rsqrt(square_sum + epsilon) * GRAM_SCALE
        for load in loads:
            load.wait()
        for b in range(blocks):
            column = jnp.broadcast_to(norm[b : b + 1, :], (rows, rows)).T
            for s in range(slots):
                at = slice(s * terms, (s + 1) * terms)
                left_ref[b, :, at] = (weight_ref[b, :, at] * column).astype(jnp.bfloat16)

        def multiply(step, carry):
            for p in range(UNROLL):
                k = step * UNROLL + p
                pltpu.make_async_copy(
                    piece_refs[0].at[pl.ds(0, slots * terms)], tile_buf.at[k], arrived.at[k]
                ).wait()
            for p in range(UNROLL):
                k = step * UNROLL + p
                left = pair_ref[first + k, 0] - doc_at * blocks
                right_block = pair_ref[first + k, 1] % blocks
                _, _, right_doc = place_right(pair_ref[first + k, 1] // blocks, doc_at)
                id_row = right_doc * own_slots // rows
                id_at = right_doc * own_slots % rows + right_block * slots
                len_row = length_ref[right_doc, pl.ds(right_block, 1), :]
                parts = []
                for i in range(slots):
                    wanted = own_ref[left, i]
                    found = jnp.int32(0)
                    place = jnp.int32(0)
                    for j in range(slots):
                        same = ids_ref[id_row, id_at + j] == wanted
                        found = jnp.where(same, 1, found)
                        place = jnp.where(same, j, place)
                    start = pl.multiple_of(place * terms, terms)
                    c = tile_buf[k, pl.ds(start, terms), :].astype(jnp.float32)
                    factor = found.astype(jnp.float32) / (c + len_row)
                    parts.append((c * idf_ref[left * slots + i] * factor).astype(jnp.bfloat16))
                right_tile = jnp.concatenate(parts, axis=0)
                gram = jnp.dot(left_ref[left], right_tile, preferred_element_type=jnp.float32)
                for g in range(n_term):
                    gram_ref[place_owner(g, term_at), k] = gram[g * part : (g + 1) * part]
            span = pl.ds(step * UNROLL, UNROLL)
            pltpu.make_async_copy(
                gram_ref.at[:, span], out_hbm.at[:, span], written.at[step]
            ).start()
            return carry

        lax.fori_loop(0, groups, multiply, 0)

        def drain(step, carry):
            span = pl.ds(step * UNROLL, UNROLL)
            pltpu.make_async_copy(
                gram_ref.at[:, span], out_hbm.at[:, span], written.at[step]
            ).wait()
            return carry

        lax.fori_loop(0, groups, drain, 0)

    smem = pl.BlockSpec(memory_space=pltpu.SMEM)
    vmem = pl.BlockSpec(memory_space=pltpu.VMEM)
    anywhere = pl.BlockSpec(memory_space=pl.ANY)
    return pl.pallas_call(
        kernel,
        in_specs=[smem] * 3 + [vmem] * n_term + [anywhere] * (3 + len(pieces)),
        out_specs=anywhere,
        out_shape=jax.ShapeDtypeStruct((n_term, size, part, rows), jnp.float32),
        scratch_shapes=[
            pltpu.VMEM(weight.shape, jnp.float32),
            pltpu.VMEM(idf_tiles.shape, jnp.float32),
            pltpu.VMEM(len_rows.shape, jnp.float32),
            pltpu.VMEM(weight.shape, jnp.bfloat16),
            pltpu.VMEM((size, slots * terms, rows), jnp.bfloat16),
            pltpu.VMEM((n_term, size, part, rows), jnp.float32),
            pltpu.SemaphoreType.DMA((3,)),
            pltpu.SemaphoreType.DMA((size,)),
            pltpu.SemaphoreType.DMA((groups,)),
        ],
        name="gram",
    )(pairs, own_ids, all_ids, *squares, weight, idf_tiles, len_rows, *pieces)


def whole(counts, block_ids, live_slots, lengths, pairs, pair_count):
    blocks, slots, rows, terms = counts.shape
    n_doc = lax.axis_size("doc")
    n_term = lax.axis_size("term")
    doc_at = lax.axis_index("doc")
    tile_rows = blocks * slots * terms

    payload, own_counts = prepare(counts, block_ids, live_slots, lengths)
    ring = [payload] + [from_ring(payload, 0, s) for s in (1, 2, 3)]
    low = jnp.concatenate(ring[:2], axis=0)
    high = jnp.concatenate(ring[2:], axis=0)
    small_ring = jnp.stack([piece[tile_rows:] for piece in ring])
    small_parts = [small_ring] + [from_ring(small_ring, 1, s) for s in (1, 2, 3)]
    small_parts = small_parts + [from_sibling(part) for part in small_parts]
    pieces = gather_rest(low, high)
    all_ids, len_rows, idf_tiles, weight, square_part = weigh(
        block_ids, small_parts, own_counts
    )
    squares = [square_part] + [swap_term(square_part, bit, n_term) for bit in range(1, n_term)]

    kept = []
    ready = []
    first = 0
    chosen = pairs
    for step, size in enumerate(CHUNKS):
        if step >= 2:
            chosen, _ = lax.optimization_barrier((chosen, ready[step - 2]))
        grams = gram_chunk(
            first, size, chosen, block_ids, all_ids, weight, squares, idf_tiles, len_rows, pieces
        )
        first += size
        near = swap_term(grams[2:].astype(jnp.float16), 1, n_term)
        pass_on = (grams[1] + near[1].astype(jnp.float32)).astype(jnp.float16)
        ready.append(pass_on)
        far = swap_term(pass_on, 2, n_term)
        kept.append((grams, near, far))
    early, _ = lax.optimization_barrier((tuple(kept[:-1]), ready[-1]))
    norm, _ = lax.optimization_barrier((lax.rsqrt(sum(squares) + epsilon), ready[-2]))
    norm_ring = gather_ring(norm[None], 0)
    norm_ring, _ = lax.optimization_barrier((norm_ring, ready[-1]))
    norm_rows = gather_sibling(gather_ring(norm_ring, 1))
    right = pairs[:, 1]
    _, _, right_doc = place_right(right // blocks, doc_at)
    norm_rows = norm_rows.reshape(n_doc * blocks, rows)[right_doc * blocks + right % blocks]
    live = jnp.arange(pairs.shape[0], dtype=jnp.int32) < pair_count[0]
    right_norm = jnp.where(live[:, None], norm_rows * (1.0 / GRAM_SCALE), 0.0)[:, None, :]

    def total(grams, near, far):
        return grams[0] + near[0].astype(jnp.float32) + far.astype(jnp.float32)

    last = pairs.shape[0] - CHUNKS[-1]
    result = jnp.concatenate([total(*each) for each in early], axis=0)
    result = jnp.pad(result, ((0, CHUNKS[-1]), (0, 0), (0, 0))) * right_norm
    result, final = lax.optimization_barrier((result, kept[-1]))
    return result.at[last:].set(total(*final) * right_norm[last:])


def solution(mesh):
    in_specs = (
        P("doc", "term", None, None),
        P("doc", "term"),
        P("doc", "term"),
        P("doc"),
        P(("doc", "pair"), None),
        P(("doc", "pair")),
    )
    out_specs = P(("doc", "pair"), "term", None)
    return jax.shard_map(whole, mesh=mesh, in_specs=in_specs, out_specs=out_specs, check_vma=False)
```

```python
import jax
import jax.numpy as jnp
from jax import lax
from jax.experimental import pallas as pl
from jax.experimental.pallas import tpu as pltpu
from jax.sharding import PartitionSpec as P


SIDE = 4
CORES = 2
UNROLL = 4
CHUNKS = (24, 24, 16)
ROOT_SCALE = 64.0
SMALL_ROWS = 32

saturation = 1.2
length_weight = 0.75
epsilon = 1e-06


def doc_of(y, x, core):
    return ((y % SIDE) * SIDE + x % SIDE) * CORES + core % CORES


def permute_doc(value, source):
    moves = [
        (doc_of(*source(y, x, c)), doc_of(y, x, c))
        for y in range(SIDE)
        for x in range(SIDE)
        for c in range(CORES)
    ]
    return lax.ppermute(value, "doc", moves)


def from_sibling(value):
    return permute_doc(value, lambda y, x, c: (y, x, c + 1))


def from_ring(value, phase, shift):
    def source(y, x, c):
        return (y, x + shift, c) if c == phase else (y + shift, x, c)

    return permute_doc(value, source)


def gather_ring(value, phase):
    return jnp.concatenate([value] + [from_ring(value, phase, s) for s in (1, 2, 3)], axis=0)


def gather_sibling(value):
    return jnp.concatenate([value, from_sibling(value)], axis=0)


def gather_rest(low, high):
    ahead_low = from_ring(low, 1, 1)
    behind_high = from_ring(high, 1, 3)
    ahead_high = from_ring(high, 1, 1)
    behind_low = from_ring(low, 1, 3)
    across_low = from_ring(ahead_low, 1, 1)
    across_high = from_ring(behind_high, 1, 3)
    early = [low, high]
    late = [ahead_low, ahead_high, across_low, across_high, behind_low, behind_high]
    early_far = [from_sibling(piece) for piece in early]
    late_far = [from_sibling(piece) for piece in late]
    return early + late + early_far + late_far


def place_right(doc, doc_at):
    dx = ((doc >> 1) - (doc_at >> 1)) & (SIDE - 1)
    dy = ((doc >> 3) - (doc_at >> 3)) & (SIDE - 1)
    dcore = (doc ^ doc_at) & (CORES - 1)
    inner = jnp.where((doc & 1) == 0, dx, dy)
    outer = jnp.where((doc & 1) == 0, dy, dx)
    plane = (dcore << 2) | outer
    return (plane << 1) | (inner >> 1), inner & 1, (plane << 2) | inner


def pack_root(value):
    return (jnp.sqrt(value) * ROOT_SCALE).astype(jnp.float16)


def unpack_root(value):
    root = value.astype(jnp.float32) * (1.0 / ROOT_SCALE)
    return root * root


def place_owner(owner, term_at):
    apart = owner ^ term_at
    return ((apart & 1) << 1) | (apart >> 1)


def swap_term(value, bit, n_term):
    return lax.ppermute(value, "term", [(a, a ^ bit) for a in range(n_term)])


def prepare(counts, block_ids, live_slots, lengths):
    blocks, slots, rows, terms = counts.shape
    own_slots = blocks * slots
    tile_rows = own_slots * terms

    def kernel(ids_ref, live_ref, length_ref, count_ref, payload_ref, own_ref):
        cols = []
        id_rows = []
        for b in range(blocks):
            for s in range(slots):
                c = jnp.where(live_ref[b, s] > 0, count_ref[b, s], 0).astype(jnp.float32)
                at = (b * slots + s) * terms
                payload_ref[at : at + terms, :] = c.T.astype(jnp.bfloat16)
                own_ref[b, :, s * terms : (s + 1) * terms] = c.astype(jnp.bfloat16)
                cols.append(jnp.sum(jnp.where(c > 0.0, 1.0, 0.0), axis=0, keepdims=True))
                id_rows.append(jnp.full((1, rows), ids_ref[b, s], jnp.int32))
        ids = jnp.concatenate(id_rows, axis=0)
        length = length_ref[...]
        halves = lambda whole: ((whole >> 8).astype(jnp.float32), (whole & 255).astype(jnp.float32))
        spare = jnp.zeros((SMALL_ROWS - 3 * own_slots - 2 * blocks, rows), jnp.float32)
        small = jnp.concatenate(cols + [*halves(ids), *halves(length), spare], axis=0)
        payload_ref[tile_rows:, :] = small.astype(jnp.bfloat16)

    smem = pl.BlockSpec(memory_space=pltpu.SMEM)
    vmem = pl.BlockSpec(memory_space=pltpu.VMEM)
    return pl.pallas_call(
        kernel,
        in_specs=[smem, smem, vmem, vmem],
        out_specs=[vmem, vmem],
        out_shape=[
            jax.ShapeDtypeStruct((tile_rows + SMALL_ROWS, rows), jnp.bfloat16),
            jax.ShapeDtypeStruct((blocks, rows, slots * terms), jnp.bfloat16),
        ],
        name="prepare",
    )(block_ids, live_slots, lengths.reshape(blocks, rows), counts)


def weigh(block_ids, small_parts, own_counts):
    blocks, rows, width = own_counts.shape
    slots = block_ids.shape[1]
    terms = width // slots
    own_slots = blocks * slots
    n_doc = len(small_parts) * small_parts[0].shape[0]
    docs_all = n_doc * blocks * rows

    def kernel(ids_ref, own_ref, *refs):
        small_refs = refs[: len(small_parts)]
        id_ref, length_ref, idf_ref, left_ref, stat_ref = refs[len(small_parts) :]
        small = jnp.concatenate([ref[...].astype(jnp.float32) for ref in small_refs], axis=0)
        cols = small[:, :own_slots]
        ids = small[:, own_slots : 2 * own_slots] * 256.0 + small[:, 2 * own_slots : 3 * own_slots]
        flat = ids.reshape(n_doc * own_slots, rows)
        for h in range(n_doc * own_slots // rows):
            turned = flat[h * rows : (h + 1) * rows].T
            id_ref[h : h + 1, :] = turned[:1].astype(jnp.int32)
        ids = ids.astype(jnp.int32)
        packed = small[:, 3 * own_slots :]
        length = packed * 256.0 + pltpu.roll(packed, packed.shape[1] - blocks, 1)
        row_at = lax.broadcasted_iota(jnp.int32, length.shape, 1)
        total = jnp.sum(jnp.sum(jnp.where(row_at < blocks, length, 0.0), axis=0), keepdims=True)
        avg_len = total / docs_all
        scaled = saturation * (1.0 - length_weight + length_weight * length / avg_len[None])
        length_ref[...] = scaled
        for b in range(blocks):
            own_len = jnp.broadcast_to(scaled[0, b : b + 1, :], (rows, rows)).T
            square = jnp.zeros((rows, terms), jnp.float32)
            for s in range(slots):
                here = jnp.where(ids == ids_ref[b, s], cols, 0.0)
                doc_freq = jnp.sum(jnp.sum(here, axis=0), axis=0, keepdims=True)
                inv_freq = jnp.log(1.0 + (docs_all - doc_freq + 0.5) / (doc_freq + 0.5))
                idf = inv_freq * (saturation + 1.0)
                idf_ref[b * slots + s] = jnp.broadcast_to(idf, (rows, terms)).T
                c = own_ref[b, :, s * terms : (s + 1) * terms].astype(jnp.float32)
                weight = idf * c / (c + own_len)
                left_ref[b, :, s * terms : (s + 1) * terms] = weight.astype(jnp.bfloat16)
                square = square + weight * weight
            stat_ref[b : b + 1, :] = jnp.sum(square.T, axis=0, keepdims=True)

    smem = pl.BlockSpec(memory_space=pltpu.SMEM)
    vmem = pl.BlockSpec(memory_space=pltpu.VMEM)
    return pl.pallas_call(
        kernel,
        in_specs=[smem, vmem] + [vmem] * len(small_parts),
        out_specs=[vmem] * 5,
        out_shape=[
            jax.ShapeDtypeStruct((n_doc * own_slots // rows, rows), jnp.int32),
            jax.ShapeDtypeStruct((n_doc, SMALL_ROWS - 3 * own_slots, rows), jnp.float32),
            jax.ShapeDtypeStruct((own_slots, terms, rows), jnp.float32),
            jax.ShapeDtypeStruct((blocks, rows, width), jnp.bfloat16),
            jax.ShapeDtypeStruct((blocks, rows), jnp.float32),
        ],
        name="weigh",
    )(block_ids, own_counts, *small_parts)


def gram_chunk(first, size, pairs, own_ids, all_ids, n_term, left_tiles, idf_tiles, len_rows, pieces):
    own_slots, terms, rows = idf_tiles.shape
    blocks = left_tiles.shape[0]
    slots = own_slots // blocks
    part = rows // n_term
    groups = size // UNROLL
    payload_rows = pieces[0].shape[0] // 2

    def kernel(pair_ref, own_ref, ids_ref, *refs):
        doc_at = lax.axis_index("doc")
        term_at = lax.axis_index("term")
        left_hbm, idf_hbm, length_hbm = refs[:3]
        piece_refs = refs[3 : 3 + len(pieces)]
        out_hbm, *scratch = refs[3 + len(pieces) :]
        left_ref, idf_ref, length_ref, tile_buf, gram_ref, note_ref = scratch[:6]
        loaded, arrived, written = scratch[6:]
        loads = [
            pltpu.make_async_copy(src, dst, loaded.at[n])
            for n, (src, dst) in enumerate(
                [(left_hbm, left_ref), (idf_hbm, idf_ref), (length_hbm, length_ref)]
            )
        ]
        for load in loads:
            load.start()

        def fetch(k, carry):
            right = pair_ref[first + k, 1]
            piece, spot, right_doc = place_right(right >> 1, doc_at)
            note_ref[k] = right_doc
            spot = spot * payload_rows + (right & 1) * (slots * terms)
            spot = pl.multiple_of(spot, SMALL_ROWS)
            for quad in range(len(pieces) // 4):

                @pl.when((piece >> 2) == quad)
                def _():
                    for p in range(4 * quad, 4 * quad + 4):

                        @pl.when(piece == p)
                        def _():
                            pltpu.make_async_copy(
                                piece_refs[p].at[pl.ds(spot, slots * terms)],
                                tile_buf.at[k],
                                arrived.at[k],
                            ).start()

            return carry

        lax.fori_loop(0, size, fetch, 0)
        for load in loads:
            load.wait()

        def multiply(step, carry):
            for p in range(UNROLL):
                k = step * UNROLL + p
                pltpu.make_async_copy(
                    piece_refs[0].at[pl.ds(0, slots * terms)], tile_buf.at[k], arrived.at[k]
                ).wait()
            for p in range(UNROLL):
                k = step * UNROLL + p
                left = pair_ref[first + k, 0] - doc_at * blocks
                right_block = pair_ref[first + k, 1] & 1
                right_doc = note_ref[k]
                id_row = right_doc >> 4
                id_at = ((right_doc & 15) << 3) + right_block * slots
                their_ids = [ids_ref[id_row, id_at + j] for j in range(slots)]
                len_row = length_ref[right_doc, pl.ds(right_block, 1), :]
                parts = []
                for i in range(slots):
                    wanted = own_ref[left, i]
                    found = jnp.int32(0)
                    place = jnp.int32(0)
                    for j in range(slots):
                        same = their_ids[j] == wanted
                        found = jnp.where(same, 1, found)
                        place = jnp.where(same, j, place)
                    start = pl.multiple_of(place * terms, terms)
                    c = tile_buf[k, pl.ds(start, terms), :].astype(jnp.float32)
                    factor = found.astype(jnp.float32) / (c + len_row)
                    parts.append((c * idf_ref[left * slots + i] * factor).astype(jnp.bfloat16))
                right_tile = jnp.concatenate(parts, axis=0)
                gram = jnp.dot(left_ref[left], right_tile, preferred_element_type=jnp.float32)
                for g in range(n_term):
                    gram_ref[place_owner(g, term_at), k] = gram[g * part : (g + 1) * part]
            span = pl.ds(step * UNROLL, UNROLL)
            pltpu.make_async_copy(
                gram_ref.at[:, span], out_hbm.at[:, span], written.at[step]
            ).start()
            return carry

        lax.fori_loop(0, groups, multiply, 0)

        def drain(step, carry):
            span = pl.ds(step * UNROLL, UNROLL)
            pltpu.make_async_copy(
                gram_ref.at[:, span], out_hbm.at[:, span], written.at[step]
            ).wait()
            return carry

        lax.fori_loop(0, groups, drain, 0)

    smem = pl.BlockSpec(memory_space=pltpu.SMEM)
    anywhere = pl.BlockSpec(memory_space=pl.ANY)
    return pl.pallas_call(
        kernel,
        in_specs=[smem] * 3 + [anywhere] * (3 + len(pieces)),
        out_specs=anywhere,
        out_shape=jax.ShapeDtypeStruct((n_term, size, part, rows), jnp.float32),
        scratch_shapes=[
            pltpu.VMEM(left_tiles.shape, jnp.bfloat16),
            pltpu.VMEM(idf_tiles.shape, jnp.float32),
            pltpu.VMEM(len_rows.shape, jnp.float32),
            pltpu.VMEM((size, slots * terms, rows), jnp.bfloat16),
            pltpu.VMEM((n_term, size, part, rows), jnp.float32),
            pltpu.SMEM((size,), jnp.int32),
            pltpu.SemaphoreType.DMA((3,)),
            pltpu.SemaphoreType.DMA((size,)),
            pltpu.SemaphoreType.DMA((groups,)),
        ],
        name="gram",
    )(pairs, own_ids, all_ids, left_tiles, idf_tiles, len_rows, *pieces)


def whole(counts, block_ids, live_slots, lengths, pairs, pair_count):
    blocks, slots, rows, terms = counts.shape
    n_doc = lax.axis_size("doc")
    n_term = lax.axis_size("term")
    doc_at = lax.axis_index("doc")
    term_at = lax.axis_index("term")
    tile_rows = blocks * slots * terms

    payload, own_counts = prepare(counts, block_ids, live_slots, lengths)
    ring = [payload] + [from_ring(payload, 0, s) for s in (1, 2, 3)]
    low = jnp.concatenate(ring[:2], axis=0)
    high = jnp.concatenate(ring[2:], axis=0)
    small_ring = jnp.stack([piece[tile_rows:] for piece in ring])
    small_parts = [small_ring] + [from_ring(small_ring, 1, s) for s in (1, 2, 3)]
    small_parts = small_parts + [from_sibling(part) for part in small_parts]
    pieces = gather_rest(low, high)
    all_ids, len_rows, idf_tiles, left_tiles, stat = weigh(block_ids, small_parts, own_counts)
    stats = [stat] + [swap_term(stat, bit, n_term) for bit in range(1, n_term)]
    norm = lax.rsqrt(sum(stats) + epsilon)

    kept = []
    ready = []
    first = 0
    for size in CHUNKS:
        grams = gram_chunk(
            first, size, pairs, block_ids, all_ids, n_term, left_tiles, idf_tiles, len_rows, pieces
        )
        first += size
        near = swap_term(pack_root(grams[2:]), 1, n_term)
        pass_on = pack_root(grams[1] + unpack_root(near[1]))
        ready.append(pass_on)
        far = swap_term(pass_on, 2, n_term)
        kept.append((grams, near, far))
    early, _ = lax.optimization_barrier((tuple(kept[:-1]), ready[-1]))
    late_norm, _ = lax.optimization_barrier((norm, ready[-2]))
    norm_ring = gather_ring(late_norm[None], 0)
    norm_ring, _ = lax.optimization_barrier((norm_ring, ready[-1]))
    norm_rows = gather_sibling(gather_ring(norm_ring, 1))
    right = pairs[:, 1]
    _, _, right_doc = place_right(right // blocks, doc_at)
    norm_rows = norm_rows.reshape(n_doc * blocks, rows)[right_doc * blocks + right % blocks]
    live = jnp.arange(pairs.shape[0], dtype=jnp.int32) < pair_count[0]
    right_norm = jnp.where(live[:, None], norm_rows, 0.0)[:, None, :]
    part = rows // n_term
    own_norm = lax.dynamic_slice_in_dim(norm, term_at * part, part, 1)
    own_norm = jnp.broadcast_to(own_norm[:, :, None], (blocks, part, rows))
    left = (pairs[:, 0] - doc_at * blocks)[:, None, None]

    def total(at, grams, near, far):
        value = grams[0] + unpack_root(near[0]) + unpack_root(far)
        return value * jnp.where(left[at] == 0, own_norm[0], own_norm[1])

    ends = [sum(CHUNKS[: n + 1]) for n in range(len(CHUNKS))]
    spans = [slice(end - size, end) for end, size in zip(ends, CHUNKS)]
    result = jnp.concatenate([total(at, *each) for at, each in zip(spans, early)], axis=0)
    result = jnp.pad(result, ((0, CHUNKS[-1]), (0, 0), (0, 0))) * right_norm
    result, final = lax.optimization_barrier((result, kept[-1]))
    return result.at[spans[-1]].set(total(spans[-1], *final) * right_norm[spans[-1]])


def solution(mesh):
    in_specs = (
        P("doc", "term", None, None),
        P("doc", "term"),
        P("doc", "term"),
        P("doc"),
        P(("doc", "pair"), None),
        P(("doc", "pair")),
    )
    out_specs = P(("doc", "pair"), "term", None)
    return jax.shard_map(whole, mesh=mesh, in_specs=in_specs, out_specs=out_specs, check_vma=False)
```

```python
import jax
import jax.numpy as jnp
from jax import lax
from jax.experimental import pallas as pl
from jax.experimental.pallas import tpu as pltpu
from jax.sharding import PartitionSpec as P


SIDE = 4
CORES = 2
UNROLL = 4
CHUNKS = (24, 24, 16)
ROOT_SCALE = 64.0
SMALL_ROWS = 32

saturation = 1.2
length_weight = 0.75
epsilon = 1e-06


def doc_of(y, x, core):
    return ((y % SIDE) * SIDE + x % SIDE) * CORES + core % CORES


def permute_doc(value, source):
    moves = [
        (doc_of(*source(y, x, c)), doc_of(y, x, c))
        for y in range(SIDE)
        for x in range(SIDE)
        for c in range(CORES)
    ]
    return lax.ppermute(value, "doc", moves)


def from_sibling(value):
    return permute_doc(value, lambda y, x, c: (y, x, c + 1))


def from_ring(value, phase, shift):
    def source(y, x, c):
        return (y, x + shift, c) if c == phase else (y + shift, x, c)

    return permute_doc(value, source)


def gather_ring(value, phase):
    return jnp.concatenate([value] + [from_ring(value, phase, s) for s in (1, 2, 3)], axis=0)


def gather_sibling(value):
    return jnp.concatenate([value, from_sibling(value)], axis=0)


def gather_rest(low, high):
    ahead_low = from_ring(low, 1, 1)
    behind_high = from_ring(high, 1, 3)
    ahead_high = from_ring(high, 1, 1)
    behind_low = from_ring(low, 1, 3)
    across_low = from_ring(ahead_low, 1, 1)
    across_high = from_ring(behind_high, 1, 3)
    early = [low, high]
    late = [ahead_low, ahead_high, across_low, across_high, behind_low, behind_high]
    early_far = [from_sibling(piece) for piece in early]
    late_far = [from_sibling(piece) for piece in late]
    return early + late + early_far + late_far


def place_right(doc, doc_at):
    dx = ((doc >> 1) - (doc_at >> 1)) & (SIDE - 1)
    dy = ((doc >> 3) - (doc_at >> 3)) & (SIDE - 1)
    dcore = (doc ^ doc_at) & (CORES - 1)
    inner = jnp.where((doc & 1) == 0, dx, dy)
    outer = jnp.where((doc & 1) == 0, dy, dx)
    plane = (dcore << 2) | outer
    return (plane << 1) | (inner >> 1), inner & 1, (plane << 2) | inner


def pack_root(value):
    return (jnp.sqrt(value) * ROOT_SCALE).astype(jnp.float16)


def unpack_root(value):
    root = value.astype(jnp.float32) * (1.0 / ROOT_SCALE)
    return root * root


def place_owner(owner, term_at):
    apart = owner ^ term_at
    return ((apart & 1) << 1) | (apart >> 1)


def swap_term(value, bit, n_term):
    return lax.ppermute(value, "term", [(a, a ^ bit) for a in range(n_term)])


def prepare(counts, block_ids, live_slots, lengths):
    blocks, slots, rows, terms = counts.shape
    own_slots = blocks * slots
    tile_rows = own_slots * terms

    def kernel(ids_ref, live_ref, length_ref, count_ref, payload_ref, own_ref):
        cols = []
        id_rows = []
        for b in range(blocks):
            for s in range(slots):
                c = jnp.where(live_ref[b, s] > 0, count_ref[b, s], 0).astype(jnp.float32)
                at = (b * slots + s) * terms
                payload_ref[at : at + terms, :] = c.T.astype(jnp.bfloat16)
                own_ref[b, :, s * terms : (s + 1) * terms] = c.astype(jnp.bfloat16)
                cols.append(jnp.sum(jnp.where(c > 0.0, 1.0, 0.0), axis=0, keepdims=True))
                id_rows.append(jnp.full((1, rows), ids_ref[b, s], jnp.int32))
        ids = jnp.concatenate(id_rows, axis=0)
        length = length_ref[...]
        halves = lambda whole: ((whole >> 8).astype(jnp.float32), (whole & 255).astype(jnp.float32))
        spare = jnp.zeros((SMALL_ROWS - 3 * own_slots - 2 * blocks, rows), jnp.float32)
        small = jnp.concatenate(cols + [*halves(ids), *halves(length), spare], axis=0)
        payload_ref[tile_rows:, :] = small.astype(jnp.bfloat16)

    smem = pl.BlockSpec(memory_space=pltpu.SMEM)
    vmem = pl.BlockSpec(memory_space=pltpu.VMEM)
    return pl.pallas_call(
        kernel,
        in_specs=[smem, smem, vmem, vmem],
        out_specs=[vmem, vmem],
        out_shape=[
            jax.ShapeDtypeStruct((tile_rows + SMALL_ROWS, rows), jnp.bfloat16),
            jax.ShapeDtypeStruct((blocks, rows, slots * terms), jnp.bfloat16),
        ],
        name="prepare",
    )(block_ids, live_slots, lengths.reshape(blocks, rows), counts)


def weigh(block_ids, small_parts, own_counts):
    blocks, rows, width = own_counts.shape
    slots = block_ids.shape[1]
    terms = width // slots
    own_slots = blocks * slots
    n_doc = len(small_parts) * small_parts[0].shape[0]
    docs_all = n_doc * blocks * rows

    def kernel(ids_ref, own_ref, *refs):
        small_refs = refs[: len(small_parts)]
        id_ref, length_ref, idf_ref, left_ref, stat_ref = refs[len(small_parts) :]
        small = jnp.concatenate([ref[...].astype(jnp.float32) for ref in small_refs], axis=0)
        cols = small[:, :own_slots]
        ids = small[:, own_slots : 2 * own_slots] * 256.0 + small[:, 2 * own_slots : 3 * own_slots]
        flat = ids.reshape(n_doc * own_slots, rows)
        for h in range(n_doc * own_slots // rows):
            turned = flat[h * rows : (h + 1) * rows].T
            id_ref[h : h + 1, :] = turned[:1].astype(jnp.int32)
        ids = ids.astype(jnp.int32)
        packed = small[:, 3 * own_slots :]
        length = packed * 256.0 + pltpu.roll(packed, packed.shape[1] - blocks, 1)
        row_at = lax.broadcasted_iota(jnp.int32, length.shape, 1)
        total = jnp.sum(jnp.sum(jnp.where(row_at < blocks, length, 0.0), axis=0), keepdims=True)
        avg_len = total / docs_all
        scaled = saturation * (1.0 - length_weight + length_weight * length / avg_len[None])
        length_ref[...] = scaled
        for b in range(blocks):
            own_len = jnp.broadcast_to(scaled[0, b : b + 1, :], (rows, rows)).T
            square = jnp.zeros((rows, terms), jnp.float32)
            for s in range(slots):
                here = jnp.where(ids == ids_ref[b, s], cols, 0.0)
                doc_freq = jnp.sum(jnp.sum(here, axis=0), axis=0, keepdims=True)
                inv_freq = jnp.log(1.0 + (docs_all - doc_freq + 0.5) / (doc_freq + 0.5))
                idf = inv_freq * (saturation + 1.0)
                idf_ref[b * slots + s] = jnp.broadcast_to(idf, (rows, terms)).T
                c = own_ref[b, :, s * terms : (s + 1) * terms].astype(jnp.float32)
                weight = idf * c / (c + own_len)
                left_ref[b, :, s * terms : (s + 1) * terms] = weight.astype(jnp.bfloat16)
                square = square + weight * weight
            stat_ref[b : b + 1, :] = jnp.sum(square.T, axis=0, keepdims=True)

    smem = pl.BlockSpec(memory_space=pltpu.SMEM)
    vmem = pl.BlockSpec(memory_space=pltpu.VMEM)
    return pl.pallas_call(
        kernel,
        in_specs=[smem, vmem] + [vmem] * len(small_parts),
        out_specs=[vmem] * 5,
        out_shape=[
            jax.ShapeDtypeStruct((n_doc * own_slots // rows, rows), jnp.int32),
            jax.ShapeDtypeStruct((n_doc, SMALL_ROWS - 3 * own_slots, rows), jnp.float32),
            jax.ShapeDtypeStruct((own_slots, terms, rows), jnp.float32),
            jax.ShapeDtypeStruct((blocks, rows, width), jnp.bfloat16),
            jax.ShapeDtypeStruct((blocks, rows), jnp.float32),
        ],
        name="weigh",
    )(block_ids, own_counts, *small_parts)


def gram_chunk(first, size, pairs, own_ids, all_ids, n_term, left_tiles, idf_tiles, len_rows, pieces):
    own_slots, terms, rows = idf_tiles.shape
    blocks = left_tiles.shape[0]
    slots = own_slots // blocks
    part = rows // n_term
    groups = size // UNROLL
    payload_rows = pieces[0].shape[0] // 2

    def kernel(pair_ref, own_ref, ids_ref, *refs):
        doc_at = lax.axis_index("doc")
        term_at = lax.axis_index("term")
        left_hbm, idf_hbm, length_hbm = refs[:3]
        piece_refs = refs[3 : 3 + len(pieces)]
        out_hbm, *scratch = refs[3 + len(pieces) :]
        left_ref, idf_ref, length_ref, tile_buf, gram_ref, note_ref = scratch[:6]
        loaded, arrived, written = scratch[6:]
        loads = [
            pltpu.make_async_copy(src, dst, loaded.at[n])
            for n, (src, dst) in enumerate(
                [(left_hbm, left_ref), (idf_hbm, idf_ref), (length_hbm, length_ref)]
            )
        ]
        for load in loads:
            load.start()

        def fetch(k, carry):
            right = pair_ref[first + k, 1]
            piece, spot, right_doc = place_right(right >> 1, doc_at)
            note_ref[k] = right_doc
            spot = spot * payload_rows + (right & 1) * (slots * terms)
            spot = pl.multiple_of(spot, SMALL_ROWS)
            for quad in range(len(pieces) // 4):

                @pl.when((piece >> 2) == quad)
                def _():
                    for p in range(4 * quad, 4 * quad + 4):

                        @pl.when(piece == p)
                        def _():
                            pltpu.make_async_copy(
                                piece_refs[p].at[pl.ds(spot, slots * terms)],
                                tile_buf.at[k],
                                arrived.at[k],
                            ).start()

            return carry

        lax.fori_loop(0, size, fetch, 0)
        for load in loads:
            load.wait()

        def multiply(step, carry):
            for p in range(UNROLL):
                k = step * UNROLL + p
                pltpu.make_async_copy(
                    piece_refs[0].at[pl.ds(0, slots * terms)], tile_buf.at[k], arrived.at[k]
                ).wait()
            for p in range(UNROLL):
                k = step * UNROLL + p
                left = pair_ref[first + k, 0] - doc_at * blocks
                right_block = pair_ref[first + k, 1] & 1
                right_doc = note_ref[k]
                id_row = right_doc >> 4
                id_at = ((right_doc & 15) << 3) + right_block * slots
                their_ids = [ids_ref[id_row, id_at + j] for j in range(slots)]
                len_row = length_ref[right_doc, pl.ds(right_block, 1), :]
                parts = []
                for i in range(slots):
                    wanted = own_ref[left, i]
                    found = jnp.int32(0)
                    place = jnp.int32(0)
                    for j in range(slots):
                        same = their_ids[j] == wanted
                        found = jnp.where(same, 1, found)
                        place = jnp.where(same, j, place)
                    start = pl.multiple_of(place * terms, terms)
                    c = tile_buf[k, pl.ds(start, terms), :].astype(jnp.float32)
                    factor = found.astype(jnp.float32) / (c + len_row)
                    parts.append((c * idf_ref[left * slots + i] * factor).astype(jnp.bfloat16))
                right_tile = jnp.concatenate(parts, axis=0)
                gram = jnp.dot(left_ref[left], right_tile, preferred_element_type=jnp.float32)
                for g in range(n_term):
                    gram_ref[place_owner(g, term_at), k] = gram[g * part : (g + 1) * part]
            span = pl.ds(step * UNROLL, UNROLL)
            pltpu.make_async_copy(
                gram_ref.at[:, span], out_hbm.at[:, span], written.at[step]
            ).start()
            return carry

        lax.fori_loop(0, groups, multiply, 0)

        def drain(step, carry):
            span = pl.ds(step * UNROLL, UNROLL)
            pltpu.make_async_copy(
                gram_ref.at[:, span], out_hbm.at[:, span], written.at[step]
            ).wait()
            return carry

        lax.fori_loop(0, groups, drain, 0)

    smem = pl.BlockSpec(memory_space=pltpu.SMEM)
    anywhere = pl.BlockSpec(memory_space=pl.ANY)
    return pl.pallas_call(
        kernel,
        in_specs=[smem] * 3 + [anywhere] * (3 + len(pieces)),
        out_specs=anywhere,
        out_shape=jax.ShapeDtypeStruct((n_term, size, part, rows), jnp.float32),
        scratch_shapes=[
            pltpu.VMEM(left_tiles.shape, jnp.bfloat16),
            pltpu.VMEM(idf_tiles.shape, jnp.float32),
            pltpu.VMEM(len_rows.shape, jnp.float32),
            pltpu.VMEM((size, slots * terms, rows), jnp.bfloat16),
            pltpu.VMEM((n_term, size, part, rows), jnp.float32),
            pltpu.SMEM((size,), jnp.int32),
            pltpu.SemaphoreType.DMA((3,)),
            pltpu.SemaphoreType.DMA((size,)),
            pltpu.SemaphoreType.DMA((groups,)),
        ],
        name="gram",
    )(pairs, own_ids, all_ids, left_tiles, idf_tiles, len_rows, *pieces)


def whole(counts, block_ids, live_slots, lengths, pairs, pair_count):
    blocks, slots, rows, terms = counts.shape
    n_doc = lax.axis_size("doc")
    n_term = lax.axis_size("term")
    doc_at = lax.axis_index("doc")
    term_at = lax.axis_index("term")
    tile_rows = blocks * slots * terms

    payload, own_counts = prepare(counts, block_ids, live_slots, lengths)
    ring = [payload] + [from_ring(payload, 0, s) for s in (1, 2, 3)]
    low = jnp.concatenate(ring[:2], axis=0)
    high = jnp.concatenate(ring[2:], axis=0)
    small_ring = jnp.stack([piece[tile_rows:] for piece in ring])
    small_parts = [small_ring] + [from_ring(small_ring, 1, s) for s in (1, 2, 3)]
    small_parts = small_parts + [from_sibling(part) for part in small_parts]
    pieces = gather_rest(low, high)
    all_ids, len_rows, idf_tiles, left_tiles, stat = weigh(block_ids, small_parts, own_counts)
    square_pair = stat + swap_term(stat, 1, n_term)
    square_sum = square_pair + swap_term(square_pair, 2, n_term)
    norm = lax.rsqrt(square_sum + epsilon)

    kept = []
    ready = []
    first = 0
    for size in CHUNKS:
        grams = gram_chunk(
            first, size, pairs, block_ids, all_ids, n_term, left_tiles, idf_tiles, len_rows, pieces
        )
        first += size
        near = swap_term(pack_root(grams[2:]), 1, n_term)
        pass_on = pack_root(grams[1] + unpack_root(near[1]))
        ready.append(pass_on)
        far = swap_term(pass_on, 2, n_term)
        kept.append((grams, near, far))
    early, _ = lax.optimization_barrier((tuple(kept[:-1]), ready[-1]))
    late_norm, _ = lax.optimization_barrier((norm, ready[-2]))
    norm_ring = gather_ring(late_norm[None], 0)
    norm_ring, _ = lax.optimization_barrier((norm_ring, ready[-1]))
    norm_rows = gather_sibling(gather_ring(norm_ring, 1))
    right = pairs[:, 1]
    _, _, right_doc = place_right(right // blocks, doc_at)
    norm_rows = norm_rows.reshape(n_doc * blocks, rows)[right_doc * blocks + right % blocks]
    live = jnp.arange(pairs.shape[0], dtype=jnp.int32) < pair_count[0]
    right_norm = jnp.where(live[:, None], norm_rows, 0.0)[:, None, :]
    part = rows // n_term
    own_norm = lax.dynamic_slice_in_dim(norm, term_at * part, part, 1)
    own_norm = jnp.broadcast_to(own_norm[:, :, None], (blocks, part, rows))
    left = (pairs[:, 0] - doc_at * blocks)[:, None, None]

    def total(at, grams, near, far):
        value = grams[0] + unpack_root(near[0]) + unpack_root(far)
        return value * jnp.where(left[at] == 0, own_norm[0], own_norm[1])

    ends = [sum(CHUNKS[: n + 1]) for n in range(len(CHUNKS))]
    spans = [slice(end - size, end) for end, size in zip(ends, CHUNKS)]
    result = jnp.concatenate([total(at, *each) for at, each in zip(spans, early)], axis=0)
    result = jnp.pad(result, ((0, CHUNKS[-1]), (0, 0), (0, 0))) * right_norm
    result, final = lax.optimization_barrier((result, kept[-1]))
    return result.at[spans[-1]].set(total(spans[-1], *final) * right_norm[spans[-1]])


def solution(mesh):
    in_specs = (
        P("doc", "term", None, None),
        P("doc", "term"),
        P("doc", "term"),
        P("doc"),
        P(("doc", "pair"), None),
        P(("doc", "pair")),
    )
    out_specs = P(("doc", "pair"), "term", None)
    return jax.shard_map(whole, mesh=mesh, in_specs=in_specs, out_specs=out_specs, check_vma=False)
```

```python
import jax
import jax.numpy as jnp
from jax import lax
from jax.experimental import pallas as pl
from jax.experimental.pallas import tpu as pltpu
from jax.sharding import PartitionSpec as P


SIDE = 4
CORES = 2
UNROLL = 4
CHUNKS = (24, 24, 16)
GRAM_SCALE = 32.0
SMALL_ROWS = 32

saturation = 1.2
length_weight = 0.75
epsilon = 1e-06


def doc_of(y, x, core):
    return ((y % SIDE) * SIDE + x % SIDE) * CORES + core % CORES


def permute_doc(value, source):
    moves = [
        (doc_of(*source(y, x, c)), doc_of(y, x, c))
        for y in range(SIDE)
        for x in range(SIDE)
        for c in range(CORES)
    ]
    return lax.ppermute(value, "doc", moves)


def from_sibling(value):
    return permute_doc(value, lambda y, x, c: (y, x, c + 1))


def from_ring(value, phase, shift):
    def source(y, x, c):
        return (y, x + shift, c) if c == phase else (y + shift, x, c)

    return permute_doc(value, source)


def gather_rest(low, high):
    ahead_low = from_ring(low, 1, 1)
    behind_high = from_ring(high, 1, 3)
    ahead_high = from_ring(high, 1, 1)
    behind_low = from_ring(low, 1, 3)
    across_low = from_ring(ahead_low, 1, 1)
    across_high = from_ring(behind_high, 1, 3)
    early = [low, high]
    late = [ahead_low, ahead_high, across_low, across_high, behind_low, behind_high]
    early_far = [from_sibling(piece) for piece in early]
    late_far = [from_sibling(piece) for piece in late]
    return early + late + early_far + late_far


def place_right(doc, doc_at):
    dx = ((doc >> 1) - (doc_at >> 1)) & (SIDE - 1)
    dy = ((doc >> 3) - (doc_at >> 3)) & (SIDE - 1)
    dcore = (doc ^ doc_at) & (CORES - 1)
    inner = jnp.where((doc & 1) == 0, dx, dy)
    outer = jnp.where((doc & 1) == 0, dy, dx)
    plane = (dcore << 2) | outer
    return (plane << 1) | (inner >> 1), inner & 1, (plane << 2) | inner


def place_owner(owner, term_at):
    apart = owner ^ term_at
    return ((apart & 1) << 1) | (apart >> 1)


def swap_term(value, bit, n_term):
    return lax.ppermute(value, "term", [(a, a ^ bit) for a in range(n_term)])


def prepare(counts, block_ids, live_slots, lengths):
    blocks, slots, rows, terms = counts.shape
    own_slots = blocks * slots
    tile_rows = own_slots * terms

    def kernel(ids_ref, live_ref, length_ref, count_ref, payload_ref, own_ref):
        cols = []
        id_rows = []
        for b in range(blocks):
            for s in range(slots):
                c = jnp.where(live_ref[b, s] > 0, count_ref[b, s], 0).astype(jnp.float32)
                at = (b * slots + s) * terms
                payload_ref[at : at + terms, :] = c.T.astype(jnp.bfloat16)
                own_ref[b, :, s * terms : (s + 1) * terms] = c.astype(jnp.bfloat16)
                cols.append(jnp.sum(jnp.where(c > 0.0, 1.0, 0.0), axis=0, keepdims=True))
                id_rows.append(jnp.full((1, rows), ids_ref[b, s], jnp.int32))
        ids = jnp.concatenate(id_rows, axis=0)
        length = length_ref[...]
        halves = lambda whole: ((whole >> 8).astype(jnp.float32), (whole & 255).astype(jnp.float32))
        spare = jnp.zeros((SMALL_ROWS - 3 * own_slots - 2 * blocks, rows), jnp.float32)
        small = jnp.concatenate(cols + [*halves(ids), *halves(length), spare], axis=0)
        payload_ref[tile_rows:, :] = small.astype(jnp.bfloat16)

    smem = pl.BlockSpec(memory_space=pltpu.SMEM)
    vmem = pl.BlockSpec(memory_space=pltpu.VMEM)
    return pl.pallas_call(
        kernel,
        in_specs=[smem, smem, vmem, vmem],
        out_specs=[vmem, vmem],
        out_shape=[
            jax.ShapeDtypeStruct((tile_rows + SMALL_ROWS, rows), jnp.bfloat16),
            jax.ShapeDtypeStruct((blocks, rows, slots * terms), jnp.bfloat16),
        ],
        name="prepare",
    )(block_ids, live_slots, lengths.reshape(blocks, rows), counts)


def weigh(block_ids, small_parts, own_counts):
    blocks, rows, width = own_counts.shape
    slots = block_ids.shape[1]
    terms = width // slots
    own_slots = blocks * slots
    n_doc = len(small_parts) * small_parts[0].shape[0]
    docs_all = n_doc * blocks * rows

    def kernel(ids_ref, own_ref, *refs):
        small_refs = refs[: len(small_parts)]
        id_ref, length_ref, idf_ref, weight_ref, square_ref = refs[len(small_parts) :]
        small = jnp.concatenate([ref[...].astype(jnp.float32) for ref in small_refs], axis=0)
        cols = small[:, :own_slots]
        ids = small[:, own_slots : 2 * own_slots] * 256.0 + small[:, 2 * own_slots : 3 * own_slots]
        flat = ids.reshape(n_doc * own_slots, rows)
        for h in range(n_doc * own_slots // rows):
            turned = flat[h * rows : (h + 1) * rows].T
            id_ref[h : h + 1, :] = turned[:1].astype(jnp.int32)
        ids = ids.astype(jnp.int32)
        packed = small[:, 3 * own_slots :]
        length = packed * 256.0 + pltpu.roll(packed, packed.shape[1] - blocks, 1)
        row_at = lax.broadcasted_iota(jnp.int32, length.shape, 1)
        total = jnp.sum(jnp.sum(jnp.where(row_at < blocks, length, 0.0), axis=0), keepdims=True)
        avg_len = total / docs_all
        scaled = saturation * (1.0 - length_weight + length_weight * length / avg_len[None])
        length_ref[...] = scaled
        for b in range(blocks):
            own_len = jnp.broadcast_to(scaled[0, b : b + 1, :], (rows, rows)).T
            square = jnp.zeros((rows, terms), jnp.float32)
            for s in range(slots):
                here = jnp.where(ids == ids_ref[b, s], cols, 0.0)
                doc_freq = jnp.sum(jnp.sum(here, axis=0), axis=0, keepdims=True)
                inv_freq = jnp.log(1.0 + (docs_all - doc_freq + 0.5) / (doc_freq + 0.5))
                idf = inv_freq * (saturation + 1.0)
                idf_ref[b * slots + s] = jnp.broadcast_to(idf, (rows, terms)).T
                c = own_ref[b, :, s * terms : (s + 1) * terms].astype(jnp.float32)
                weight = idf * c / (c + own_len)
                weight_ref[b, :, s * terms : (s + 1) * terms] = weight
                square = square + weight * weight
            square_ref[b : b + 1, :] = jnp.sum(square.T, axis=0, keepdims=True)

    smem = pl.BlockSpec(memory_space=pltpu.SMEM)
    vmem = pl.BlockSpec(memory_space=pltpu.VMEM)
    return pl.pallas_call(
        kernel,
        in_specs=[smem, vmem] + [vmem] * len(small_parts),
        out_specs=[vmem] * 5,
        out_shape=[
            jax.ShapeDtypeStruct((n_doc * own_slots // rows, rows), jnp.int32),
            jax.ShapeDtypeStruct((n_doc, SMALL_ROWS - 3 * own_slots, rows), jnp.float32),
            jax.ShapeDtypeStruct((own_slots, terms, rows), jnp.float32),
            jax.ShapeDtypeStruct((blocks, rows, width), jnp.float32),
            jax.ShapeDtypeStruct((blocks, rows), jnp.float32),
        ],
        name="weigh",
    )(block_ids, own_counts, *small_parts)


def gram_chunk(first, size, pairs, own_ids, all_ids, weight, squares, idf_tiles, len_rows, pieces):
    own_slots, terms, rows = idf_tiles.shape
    blocks = weight.shape[0]
    slots = own_slots // blocks
    n_term = len(squares)
    part = rows // n_term
    groups = size // UNROLL
    payload_rows = pieces[0].shape[0] // 2

    def kernel(pair_ref, own_ref, ids_ref, *refs):
        doc_at = lax.axis_index("doc")
        term_at = lax.axis_index("term")
        square_refs = refs[:n_term]
        weight_hbm, idf_hbm, length_hbm = refs[n_term : n_term + 3]
        piece_refs = refs[n_term + 3 : n_term + 3 + len(pieces)]
        out_hbm, *scratch = refs[n_term + 3 + len(pieces) :]
        weight_ref, idf_ref, length_ref, left_ref, tile_buf, gram_ref, note_ref = scratch[:7]
        loaded, arrived, written = scratch[7:]
        loads = [
            pltpu.make_async_copy(src, dst, loaded.at[n])
            for n, (src, dst) in enumerate(
                [(weight_hbm, weight_ref), (idf_hbm, idf_ref), (length_hbm, length_ref)]
            )
        ]
        for load in loads:
            load.start()

        def fetch(k, carry):
            right = pair_ref[first + k, 1]
            piece, spot, right_doc = place_right(right >> 1, doc_at)
            note_ref[k] = right_doc
            spot = spot * payload_rows + (right & 1) * (slots * terms)
            spot = pl.multiple_of(spot, SMALL_ROWS)
            for quad in range(len(pieces) // 4):

                @pl.when((piece >> 2) == quad)
                def _():
                    for p in range(4 * quad, 4 * quad + 4):

                        @pl.when(piece == p)
                        def _():
                            pltpu.make_async_copy(
                                piece_refs[p].at[pl.ds(spot, slots * terms)],
                                tile_buf.at[k],
                                arrived.at[k],
                            ).start()

            return carry

        lax.fori_loop(0, size, fetch, 0)
        square_sum = square_refs[0][...]
        for ref in square_refs[1:]:
            square_sum = square_sum + ref[...]
        norm = lax.rsqrt(square_sum + epsilon) * GRAM_SCALE
        for load in loads:
            load.wait()
        for b in range(blocks):
            column = jnp.broadcast_to(norm[b : b + 1, :], (rows, rows)).T
            for s in range(slots):
                at = slice(s * terms, (s + 1) * terms)
                left_ref[b, :, at] = (weight_ref[b, :, at] * column).astype(jnp.bfloat16)

        def multiply(step, carry):
            for p in range(UNROLL):
                k = step * UNROLL + p
                pltpu.make_async_copy(
                    piece_refs[0].at[pl.ds(0, slots * terms)], tile_buf.at[k], arrived.at[k]
                ).wait()
            for p in range(UNROLL):
                k = step * UNROLL + p
                left = pair_ref[first + k, 0] - doc_at * blocks
                right_block = pair_ref[first + k, 1] & 1
                right_doc = note_ref[k]
                id_row = right_doc >> 4
                id_at = ((right_doc & 15) << 3) + right_block * slots
                their_ids = [ids_ref[id_row, id_at + j] for j in range(slots)]
                len_row = length_ref[right_doc, pl.ds(right_block, 1), :]
                parts = []
                for i in range(slots):
                    wanted = own_ref[left, i]
                    found = jnp.int32(0)
                    place = jnp.int32(0)
                    for j in range(slots):
                        same = their_ids[j] == wanted
                        found = jnp.where(same, 1, found)
                        place = jnp.where(same, j, place)
                    start = pl.multiple_of(place * terms, terms)
                    c = tile_buf[k, pl.ds(start, terms), :].astype(jnp.float32)
                    factor = found.astype(jnp.float32) / (c + len_row)
                    parts.append((c * idf_ref[left * slots + i] * factor).astype(jnp.bfloat16))
                right_tile = jnp.concatenate(parts, axis=0)
                gram = jnp.dot(left_ref[left], right_tile, preferred_element_type=jnp.float32)
                for g in range(n_term):
                    gram_ref[place_owner(g, term_at), k] = gram[g * part : (g + 1) * part]
            span = pl.ds(step * UNROLL, UNROLL)
            pltpu.make_async_copy(
                gram_ref.at[:, span], out_hbm.at[:, span], written.at[step]
            ).start()
            return carry

        lax.fori_loop(0, groups, multiply, 0)

        def drain(step, carry):
            span = pl.ds(step * UNROLL, UNROLL)
            pltpu.make_async_copy(
                gram_ref.at[:, span], out_hbm.at[:, span], written.at[step]
            ).wait()
            return carry

        lax.fori_loop(0, groups, drain, 0)

    smem = pl.BlockSpec(memory_space=pltpu.SMEM)
    vmem = pl.BlockSpec(memory_space=pltpu.VMEM)
    anywhere = pl.BlockSpec(memory_space=pl.ANY)
    return pl.pallas_call(
        kernel,
        in_specs=[smem] * 3 + [vmem] * n_term + [anywhere] * (3 + len(pieces)),
        out_specs=anywhere,
        out_shape=jax.ShapeDtypeStruct((n_term, size, part, rows), jnp.float32),
        scratch_shapes=[
            pltpu.VMEM(weight.shape, jnp.float32),
            pltpu.VMEM(idf_tiles.shape, jnp.float32),
            pltpu.VMEM(len_rows.shape, jnp.float32),
            pltpu.VMEM(weight.shape, jnp.bfloat16),
            pltpu.VMEM((size, slots * terms, rows), jnp.bfloat16),
            pltpu.VMEM((n_term, size, part, rows), jnp.float32),
            pltpu.SMEM((size,), jnp.int32),
            pltpu.SemaphoreType.DMA((3,)),
            pltpu.SemaphoreType.DMA((size,)),
            pltpu.SemaphoreType.DMA((groups,)),
        ],
        name="gram",
    )(pairs, own_ids, all_ids, *squares, weight, idf_tiles, len_rows, *pieces)


def whole(counts, block_ids, live_slots, lengths, pairs, pair_count):
    blocks, slots, rows, terms = counts.shape
    n_doc = lax.axis_size("doc")
    n_term = lax.axis_size("term")
    doc_at = lax.axis_index("doc")
    tile_rows = blocks * slots * terms

    payload, own_counts = prepare(counts, block_ids, live_slots, lengths)
    ring = [payload] + [from_ring(payload, 0, s) for s in (1, 2, 3)]
    low = jnp.concatenate(ring[:2], axis=0)
    high = jnp.concatenate(ring[2:], axis=0)
    small_ring = jnp.stack([piece[tile_rows:] for piece in ring])
    small_parts = [small_ring] + [from_ring(small_ring, 1, s) for s in (1, 2, 3)]
    small_parts = small_parts + [from_sibling(part) for part in small_parts]
    pieces = gather_rest(low, high)
    all_ids, len_rows, idf_tiles, weight, square_part = weigh(
        block_ids, small_parts, own_counts
    )
    squares = [square_part] + [swap_term(square_part, bit, n_term) for bit in range(1, n_term)]

    kept = []
    ready = []
    first = 0
    for size in CHUNKS:
        grams = gram_chunk(
            first, size, pairs, block_ids, all_ids, weight, squares, idf_tiles, len_rows, pieces
        )
        first += size
        near = swap_term(grams[2:].astype(jnp.float16), 1, n_term)
        pass_on = (grams[1] + near[1].astype(jnp.float32)).astype(jnp.float16)
        ready.append(pass_on)
        far = swap_term(pass_on, 2, n_term)
        kept.append((grams, near, far))
    early, _ = lax.optimization_barrier((tuple(kept[:-1]), ready[-1]))
    norm_rows = lax.rsqrt(sum(squares) + epsilon)[None]
    for dy, dx, dcore in ((0, 0, 1), (0, 1, 0), (0, 2, 0), (1, 0, 0), (2, 0, 0)):
        other = permute_doc(norm_rows, lambda y, x, c: (y + dy, x + dx, c + dcore))
        norm_rows = jnp.concatenate([norm_rows, other], axis=0)
    right, counted, doc_late, _ = lax.optimization_barrier(
        (pairs[:, 1], pair_count, jnp.broadcast_to(doc_at, (1,)), ready[1])
    )
    doc = right >> 1
    dx = ((doc >> 1) - (doc_late >> 1)) & (SIDE - 1)
    dy = ((doc >> 3) - (doc_late >> 3)) & (SIDE - 1)
    apart = (((dy * SIDE + dx) * CORES + ((doc ^ doc_late) & 1)) << 1) | (right & 1)
    norm_rows = norm_rows.reshape(n_doc * blocks, rows)[apart]
    live = jnp.arange(pairs.shape[0], dtype=jnp.int32) < counted[0]
    right_norm = jnp.where(live[:, None], norm_rows * (1.0 / GRAM_SCALE), 0.0)[:, None, :]

    def total(grams, near, far):
        return grams[0] + near[0].astype(jnp.float32) + far.astype(jnp.float32)

    last = pairs.shape[0] - CHUNKS[-1]
    result = jnp.concatenate([total(*each) for each in early], axis=0)
    result = jnp.pad(result, ((0, CHUNKS[-1]), (0, 0), (0, 0))) * right_norm
    result, final = lax.optimization_barrier((result, kept[-1]))
    return result.at[last:].set(total(*final) * right_norm[last:])


def solution(mesh):
    in_specs = (
        P("doc", "term", None, None),
        P("doc", "term"),
        P("doc", "term"),
        P("doc"),
        P(("doc", "pair"), None),
        P(("doc", "pair")),
    )
    out_specs = P(("doc", "pair"), "term", None)
    return jax.shard_map(whole, mesh=mesh, in_specs=in_specs, out_specs=out_specs, check_vma=False)
```

```python
import jax
import jax.numpy as jnp
from jax import lax
from jax.experimental import pallas as pl
from jax.experimental.pallas import tpu as pltpu
from jax.sharding import PartitionSpec as P


SIDE = 4
CORES = 2
UNROLL = 4
CHUNKS = (36, 28)
GRAM_SCALE = 32.0
SMALL_ROWS = 32

saturation = 1.2
length_weight = 0.75
epsilon = 1e-06


def doc_of(y, x, core):
    return ((y % SIDE) * SIDE + x % SIDE) * CORES + core % CORES


def permute_doc(value, source):
    moves = [
        (doc_of(*source(y, x, c)), doc_of(y, x, c))
        for y in range(SIDE)
        for x in range(SIDE)
        for c in range(CORES)
    ]
    return lax.ppermute(value, "doc", moves)


def from_sibling(value):
    return permute_doc(value, lambda y, x, c: (y, x, c + 1))


def from_ring(value, phase, shift):
    def source(y, x, c):
        return (y, x + shift, c) if c == phase else (y + shift, x, c)

    return permute_doc(value, source)


def gather_rest(low, high):
    ahead_low = from_ring(low, 1, 1)
    behind_high = from_ring(high, 1, 3)
    ahead_high = from_ring(high, 1, 1)
    behind_low = from_ring(low, 1, 3)
    across_low = from_ring(ahead_low, 1, 1)
    across_high = from_ring(behind_high, 1, 3)
    early = [low, high]
    late = [ahead_low, ahead_high, across_low, across_high, behind_low, behind_high]
    early_far = [from_sibling(piece) for piece in early]
    late_far = [from_sibling(piece) for piece in late]
    return early + late + early_far + late_far


def place_right(doc, doc_at):
    dx = ((doc >> 1) - (doc_at >> 1)) & (SIDE - 1)
    dy = ((doc >> 3) - (doc_at >> 3)) & (SIDE - 1)
    dcore = (doc ^ doc_at) & (CORES - 1)
    inner = jnp.where((doc & 1) == 0, dx, dy)
    outer = jnp.where((doc & 1) == 0, dy, dx)
    plane = (dcore << 2) | outer
    return (plane << 1) | (inner >> 1), inner & 1, (plane << 2) | inner


def place_owner(owner, term_at):
    apart = owner ^ term_at
    return ((apart & 1) << 1) | (apart >> 1)


def swap_term(value, bit, n_term):
    return lax.ppermute(value, "term", [(a, a ^ bit) for a in range(n_term)])


def prepare(counts, block_ids, live_slots, lengths):
    blocks, slots, rows, terms = counts.shape
    own_slots = blocks * slots
    tile_rows = own_slots * terms

    def kernel(ids_ref, live_ref, length_ref, count_ref, payload_ref, own_ref):
        cols = []
        id_rows = []
        for b in range(blocks):
            for s in range(slots):
                c = jnp.where(live_ref[b, s] > 0, count_ref[b, s], 0).astype(jnp.float32)
                at = (b * slots + s) * terms
                payload_ref[at : at + terms, :] = c.T.astype(jnp.bfloat16)
                own_ref[b, :, s * terms : (s + 1) * terms] = c.astype(jnp.bfloat16)
                cols.append(jnp.sum(jnp.where(c > 0.0, 1.0, 0.0), axis=0, keepdims=True))
                id_rows.append(jnp.full((1, rows), ids_ref[b, s], jnp.int32))
        ids = jnp.concatenate(id_rows, axis=0)
        length = length_ref[...]
        halves = lambda whole: ((whole >> 8).astype(jnp.float32), (whole & 255).astype(jnp.float32))
        spare = jnp.zeros((SMALL_ROWS - 3 * own_slots - 2 * blocks, rows), jnp.float32)
        small = jnp.concatenate(cols + [*halves(ids), *halves(length), spare], axis=0)
        payload_ref[tile_rows:, :] = small.astype(jnp.bfloat16)

    smem = pl.BlockSpec(memory_space=pltpu.SMEM)
    vmem = pl.BlockSpec(memory_space=pltpu.VMEM)
    return pl.pallas_call(
        kernel,
        in_specs=[smem, smem, vmem, vmem],
        out_specs=[vmem, vmem],
        out_shape=[
            jax.ShapeDtypeStruct((tile_rows + SMALL_ROWS, rows), jnp.bfloat16),
            jax.ShapeDtypeStruct((blocks, rows, slots * terms), jnp.bfloat16),
        ],
        name="prepare",
    )(block_ids, live_slots, lengths.reshape(blocks, rows), counts)


def weigh(block_ids, small_parts, own_counts):
    blocks, rows, width = own_counts.shape
    slots = block_ids.shape[1]
    terms = width // slots
    own_slots = blocks * slots
    n_doc = len(small_parts) * small_parts[0].shape[0]
    docs_all = n_doc * blocks * rows

    def kernel(ids_ref, own_ref, *refs):
        small_refs = refs[: len(small_parts)]
        id_ref, length_ref, idf_ref, weight_ref, square_ref = refs[len(small_parts) :]
        small = jnp.concatenate([ref[...].astype(jnp.float32) for ref in small_refs], axis=0)
        cols = small[:, :own_slots]
        ids = small[:, own_slots : 2 * own_slots] * 256.0 + small[:, 2 * own_slots : 3 * own_slots]
        flat = ids.reshape(n_doc * own_slots, rows)
        for h in range(n_doc * own_slots // rows):
            turned = flat[h * rows : (h + 1) * rows].T
            id_ref[h : h + 1, :] = turned[:1].astype(jnp.int32)
        ids = ids.astype(jnp.int32)
        packed = small[:, 3 * own_slots :]
        length = packed * 256.0 + pltpu.roll(packed, packed.shape[1] - blocks, 1)
        row_at = lax.broadcasted_iota(jnp.int32, length.shape, 1)
        total = jnp.sum(jnp.sum(jnp.where(row_at < blocks, length, 0.0), axis=0), keepdims=True)
        avg_len = total / docs_all
        scaled = saturation * (1.0 - length_weight + length_weight * length / avg_len[None])
        length_ref[...] = scaled
        for b in range(blocks):
            own_len = jnp.broadcast_to(scaled[0, b : b + 1, :], (rows, rows)).T
            square = jnp.zeros((rows, terms), jnp.float32)
            for s in range(slots):
                here = jnp.where(ids == ids_ref[b, s], cols, 0.0)
                doc_freq = jnp.sum(jnp.sum(here, axis=0), axis=0, keepdims=True)
                inv_freq = jnp.log(1.0 + (docs_all - doc_freq + 0.5) / (doc_freq + 0.5))
                idf = inv_freq * (saturation + 1.0)
                idf_ref[b * slots + s] = jnp.broadcast_to(idf, (rows, terms)).T
                c = own_ref[b, :, s * terms : (s + 1) * terms].astype(jnp.float32)
                weight = idf * c / (c + own_len)
                weight_ref[b, :, s * terms : (s + 1) * terms] = weight
                square = square + weight * weight
            square_ref[b : b + 1, :] = jnp.sum(square.T, axis=0, keepdims=True)

    smem = pl.BlockSpec(memory_space=pltpu.SMEM)
    vmem = pl.BlockSpec(memory_space=pltpu.VMEM)
    return pl.pallas_call(
        kernel,
        in_specs=[smem, vmem] + [vmem] * len(small_parts),
        out_specs=[vmem] * 5,
        out_shape=[
            jax.ShapeDtypeStruct((n_doc * own_slots // rows, rows), jnp.int32),
            jax.ShapeDtypeStruct((n_doc, SMALL_ROWS - 3 * own_slots, rows), jnp.float32),
            jax.ShapeDtypeStruct((own_slots, terms, rows), jnp.float32),
            jax.ShapeDtypeStruct((blocks, rows, width), jnp.float32),
            jax.ShapeDtypeStruct((blocks, rows), jnp.float32),
        ],
        name="weigh",
    )(block_ids, own_counts, *small_parts)


def gram_chunk(first, size, pairs, own_ids, all_ids, weight, squares, idf_tiles, len_rows, pieces):
    own_slots, terms, rows = idf_tiles.shape
    blocks = weight.shape[0]
    slots = own_slots // blocks
    n_term = len(squares)
    part = rows // n_term
    groups = size // UNROLL
    payload_rows = pieces[0].shape[0] // 2

    def kernel(pair_ref, own_ref, ids_ref, *refs):
        doc_at = lax.axis_index("doc")
        term_at = lax.axis_index("term")
        square_refs = refs[:n_term]
        weight_hbm, idf_hbm, length_hbm = refs[n_term : n_term + 3]
        piece_refs = refs[n_term + 3 : n_term + 3 + len(pieces)]
        out_hbm, *scratch = refs[n_term + 3 + len(pieces) :]
        weight_ref, idf_ref, length_ref, left_ref, tile_buf, gram_ref, note_ref = scratch[:7]
        loaded, arrived, written = scratch[7:]
        loads = [
            pltpu.make_async_copy(src, dst, loaded.at[n])
            for n, (src, dst) in enumerate(
                [(weight_hbm, weight_ref), (idf_hbm, idf_ref), (length_hbm, length_ref)]
            )
        ]
        for load in loads:
            load.start()

        def fetch(k, carry):
            right = pair_ref[first + k, 1]
            piece, spot, right_doc = place_right(right >> 1, doc_at)
            note_ref[k] = right_doc
            spot = spot * payload_rows + (right & 1) * (slots * terms)
            spot = pl.multiple_of(spot, SMALL_ROWS)
            for quad in range(len(pieces) // 4):

                @pl.when((piece >> 2) == quad)
                def _():
                    for p in range(4 * quad, 4 * quad + 4):

                        @pl.when(piece == p)
                        def _():
                            pltpu.make_async_copy(
                                piece_refs[p].at[pl.ds(spot, slots * terms)],
                                tile_buf.at[k],
                                arrived.at[k],
                            ).start()

            return carry

        lax.fori_loop(0, size, fetch, 0)
        square_sum = square_refs[0][...]
        for ref in square_refs[1:]:
            square_sum = square_sum + ref[...]
        norm = lax.rsqrt(square_sum + epsilon) * GRAM_SCALE
        for load in loads:
            load.wait()
        for b in range(blocks):
            column = jnp.broadcast_to(norm[b : b + 1, :], (rows, rows)).T
            for s in range(slots):
                at = slice(s * terms, (s + 1) * terms)
                left_ref[b, :, at] = (weight_ref[b, :, at] * column).astype(jnp.bfloat16)

        def multiply(step, carry):
            for p in range(UNROLL):
                k = step * UNROLL + p
                pltpu.make_async_copy(
                    piece_refs[0].at[pl.ds(0, slots * terms)], tile_buf.at[k], arrived.at[k]
                ).wait()
            for p in range(UNROLL):
                k = step * UNROLL + p
                left = pair_ref[first + k, 0] - doc_at * blocks
                right_block = pair_ref[first + k, 1] & 1
                right_doc = note_ref[k]
                id_row = right_doc >> 4
                id_at = ((right_doc & 15) << 3) + right_block * slots
                their_ids = [ids_ref[id_row, id_at + j] for j in range(slots)]
                len_row = length_ref[right_doc, pl.ds(right_block, 1), :]
                parts = []
                for i in range(slots):
                    wanted = own_ref[left, i]
                    found = jnp.int32(0)
                    place = jnp.int32(0)
                    for j in range(slots):
                        same = their_ids[j] == wanted
                        found = jnp.where(same, 1, found)
                        place = jnp.where(same, j, place)
                    start = pl.multiple_of(place * terms, terms)
                    c = tile_buf[k, pl.ds(start, terms), :].astype(jnp.float32)
                    factor = found.astype(jnp.float32) / (c + len_row)
                    parts.append((c * idf_ref[left * slots + i] * factor).astype(jnp.bfloat16))
                right_tile = jnp.concatenate(parts, axis=0)
                gram = jnp.dot(left_ref[left], right_tile, preferred_element_type=jnp.float32)
                for g in range(n_term):
                    gram_ref[place_owner(g, term_at), k] = gram[g * part : (g + 1) * part]
            span = pl.ds(step * UNROLL, UNROLL)
            pltpu.make_async_copy(
                gram_ref.at[:, span], out_hbm.at[:, span], written.at[step]
            ).start()
            return carry

        lax.fori_loop(0, groups, multiply, 0)

        def drain(step, carry):
            span = pl.ds(step * UNROLL, UNROLL)
            pltpu.make_async_copy(
                gram_ref.at[:, span], out_hbm.at[:, span], written.at[step]
            ).wait()
            return carry

        lax.fori_loop(0, groups, drain, 0)

    smem = pl.BlockSpec(memory_space=pltpu.SMEM)
    vmem = pl.BlockSpec(memory_space=pltpu.VMEM)
    anywhere = pl.BlockSpec(memory_space=pl.ANY)
    return pl.pallas_call(
        kernel,
        in_specs=[smem] * 3 + [vmem] * n_term + [anywhere] * (3 + len(pieces)),
        out_specs=anywhere,
        out_shape=jax.ShapeDtypeStruct((n_term, size, part, rows), jnp.float32),
        scratch_shapes=[
            pltpu.VMEM(weight.shape, jnp.float32),
            pltpu.VMEM(idf_tiles.shape, jnp.float32),
            pltpu.VMEM(len_rows.shape, jnp.float32),
            pltpu.VMEM(weight.shape, jnp.bfloat16),
            pltpu.VMEM((size, slots * terms, rows), jnp.bfloat16),
            pltpu.VMEM((n_term, size, part, rows), jnp.float32),
            pltpu.SMEM((size,), jnp.int32),
            pltpu.SemaphoreType.DMA((3,)),
            pltpu.SemaphoreType.DMA((size,)),
            pltpu.SemaphoreType.DMA((groups,)),
        ],
        name="gram",
    )(pairs, own_ids, all_ids, *squares, weight, idf_tiles, len_rows, *pieces)


def whole(counts, block_ids, live_slots, lengths, pairs, pair_count):
    blocks, slots, rows, terms = counts.shape
    n_doc = lax.axis_size("doc")
    n_term = lax.axis_size("term")
    doc_at = lax.axis_index("doc")
    tile_rows = blocks * slots * terms

    payload, own_counts = prepare(counts, block_ids, live_slots, lengths)
    ring = [payload] + [from_ring(payload, 0, s) for s in (1, 2, 3)]
    low = jnp.concatenate(ring[:2], axis=0)
    high = jnp.concatenate(ring[2:], axis=0)
    small_ring = jnp.stack([piece[tile_rows:] for piece in ring])
    small_parts = [small_ring] + [from_ring(small_ring, 1, s) for s in (1, 2, 3)]
    small_parts = small_parts + [from_sibling(part) for part in small_parts]
    pieces = gather_rest(low, high)
    all_ids, len_rows, idf_tiles, weight, square_part = weigh(
        block_ids, small_parts, own_counts
    )
    squares = [square_part] + [swap_term(square_part, bit, n_term) for bit in range(1, n_term)]

    kept = []
    ready = []
    first = 0
    for size in CHUNKS:
        grams = gram_chunk(
            first, size, pairs, block_ids, all_ids, weight, squares, idf_tiles, len_rows, pieces
        )
        first += size
        near = swap_term(grams[2:].astype(jnp.float16), 1, n_term)
        pass_on = (grams[1] + near[1].astype(jnp.float32)).astype(jnp.float16)
        ready.append(pass_on)
        far = swap_term(pass_on, 2, n_term)
        kept.append((grams, near, far))
    late_squares, late_pairs, counted, doc_late, _ = lax.optimization_barrier(
        (squares, pairs, pair_count, jnp.broadcast_to(doc_at, (1,)), kept[0][0])
    )
    norm_rows = lax.rsqrt(sum(late_squares) + epsilon)[None]
    for dy, dx, dcore in ((0, 0, 1), (0, 1, 0), (0, 2, 0), (1, 0, 0), (2, 0, 0)):
        other = permute_doc(norm_rows, lambda y, x, c: (y + dy, x + dx, c + dcore))
        norm_rows = jnp.concatenate([norm_rows, other], axis=0)
    right = late_pairs[:, 1]
    doc = right >> 1
    dx = ((doc >> 1) - (doc_late >> 1)) & (SIDE - 1)
    dy = ((doc >> 3) - (doc_late >> 3)) & (SIDE - 1)
    apart = (((dy * SIDE + dx) * CORES + ((doc ^ doc_late) & 1)) << 1) | (right & 1)
    norm_rows = norm_rows.reshape(n_doc * blocks, rows)[apart]
    live = jnp.arange(pairs.shape[0], dtype=jnp.int32) < counted[0]
    right_norm = jnp.where(live[:, None], norm_rows * (1.0 / GRAM_SCALE), 0.0)[:, None, :]
    early, _ = lax.optimization_barrier((tuple(kept[:-1]), ready[-1]))
    totals = [
        grams[0] + near[0].astype(jnp.float32) + far.astype(jnp.float32)
        for grams, near, far in (*early, kept[-1])
    ]
    return jnp.concatenate(totals, axis=0) * right_norm


def solution(mesh):
    in_specs = (
        P("doc", "term", None, None),
        P("doc", "term"),
        P("doc", "term"),
        P("doc"),
        P(("doc", "pair"), None),
        P(("doc", "pair")),
    )
    out_specs = P(("doc", "pair"), "term", None)
    return jax.shard_map(whole, mesh=mesh, in_specs=in_specs, out_specs=out_specs, check_vma=False)
```
